256 devices in a mesh: mass: 64 (over z, x, core), sub: 4 (over y).
Axes of the slice: x: 4, y: 4, z: 8, core: 2. Of those that a mesh axis runs over, the one named last changes fastest.
Arguments:
- queries: bfloat16 [1024, 32, 1024], P('mass'), may hold values from -6 to 6
- query_mass: int32 [1024, 32], P('mass'), may hold values from 0 to 47
- first_range: int32 [1024], P('mass'), may hold values from 0 to 61, as said below
- library: bfloat16 [32768, 1024], P(('mass', 'sub')), may hold values from -6 to 6
- library_mass: int32 [32768], P(('mass', 'sub')), may hold values from 0 to 15, as said below
- shuffle: int32 [1024], replicated, may hold values from 0 to 1023, each once
Outputs:
- target_best: float32 [1024, 5, 32], P('mass')
- decoy_best: float32 [1024, 5, 32], P('mass')
The draws below stay inside these ranges and needn't reach their ends.
Inputs may be any that keep to these rules, and one draw needn't show every extreme that they name: Within each aligned run of 16 blocks the mass ranges first_range to first_range + 2 of different blocks are disjoint. `library_mass`: every mass range holds exactly 32 spectra at each bin.
All inputs are finite; a program needn't handle non-finite values.
Results may differ from the reference program's by a relative error of at most 0.0003.
Values may be sent and summed in bfloat16 or wider, within the bound.
A program may use at most 64 MiB of HBM per device.

```python
import jax
import jax.numpy as jnp
from jax import lax

D = 1024
QUERY_ROWS = 32
BINS = 16
TOLERANCE = 4
WINDOW = 3
TOP_HITS = 5
GROUP_BLOCKS = 16
BLOCKS = 1024
RANGE_ROWS = 512
LIBRARY_ROWS = 32768
N_MASS = 64


def range_layout(key):
    spare = N_MASS - WINDOW * GROUP_BLOCKS
    total = GROUP_BLOCKS + spare
    order = jax.random.permutation(key, total)
    marked = jnp.zeros((total,), jnp.int32).at[order[:GROUP_BLOCKS]].set(1)
    position = jnp.arange(total, dtype=jnp.int32)
    before = jnp.cumsum(marked) - marked
    starts = position + (WINDOW - 1) * before
    chosen = jnp.argsort(1 - marked, stable=True)[:GROUP_BLOCKS]
    return starts[chosen]


def draw_first_range(key, part):
    shared = range_layout(jax.random.fold_in(key, 7))

    def one_group(group):
        own = range_layout(jax.random.fold_in(jax.random.fold_in(key, 11), group))
        use_shared = jax.random.randint(jax.random.fold_in(jax.random.fold_in(key, 13), group), (), 0, 2)
        starts = jnp.where(use_shared == 1, shared, own)
        order = jax.random.permutation(jax.random.fold_in(jax.random.fold_in(key, 17), group), GROUP_BLOCKS)
        return starts[order]
    groups = jnp.arange(N_MASS, dtype=jnp.int32)
    return jax.vmap(one_group)(groups).reshape(-1).astype(jnp.int32)


def draw_library_mass(key, part):

    def one_range(index):
        order = jax.random.permutation(jax.random.fold_in(key, index), RANGE_ROWS)
        return order % BINS
    ranges = jnp.arange(N_MASS, dtype=jnp.int32)
    return jax.vmap(one_range)(ranges).reshape(-1).astype(jnp.int32)


def place_ends(values, own_key, smallest, high):
    longest = values.shape.index(max(values.shape))
    spots = []
    for shift in (0, 1):
        where = [jax.random.randint(jax.random.fold_in(own_key, axis), (), 0, length) for axis, length in enumerate(values.shape)]
        where[longest] = (where[longest] + shift) % values.shape[longest]
        spots.append(tuple(where))
    return values.at[spots[0]].set(smallest).at[spots[1]].set(high)


def levels(key, shape, pieces, low, largest):
    loudness, own = 1.0, jax.random.fold_in(key, 6)
    for axis_at, parts in pieces:
        heights = jnp.exp(jax.random.uniform(jax.random.fold_in(own, axis_at), (parts,), jnp.float32, low / len(pieces), largest / len(pieces)))
        loudness = loudness * jnp.repeat(heights, shape[axis_at] // parts).reshape([-1 if axis == axis_at else 1 for axis in range(len(shape))])
    return loudness


def bell_draw(own_key, extent, width, most, split=(), kind=jnp.bfloat16):
    level = levels(own_key, extent, split, -0.22, 0.18) if split else 1.0
    array = jax.random.normal(own_key, extent, jnp.float32) * width * level
    return jnp.minimum(jnp.maximum(array, -most), most).astype(kind)


def setup_inputs(seed: int = 0) -> dict:
    key_of = jax.random.split(jax.random.key(seed), 7)
    queries = bell_draw(key_of[0], (BLOCKS, QUERY_ROWS, D), 1.0, 6.0, ((0, 64),))
    query_mass = place_ends(jax.random.randint(key_of[1], (BLOCKS, QUERY_ROWS), 0, WINDOW * BINS), jax.random.fold_in(key_of[1], 1), 0, (WINDOW * BINS) - 1).astype(jnp.int32)
    first_range = draw_first_range(jax.random.fold_in(key_of[6], 71), 0)
    library = bell_draw(key_of[3], (LIBRARY_ROWS, D), 1.0, 6.0, ((0, 256),))
    library_mass = draw_library_mass(jax.random.fold_in(key_of[6], 71), 0)
    shuffle = jax.random.permutation(key_of[5], D).astype(jnp.int32)
    return {"queries": queries, "query_mass": query_mass, "first_range": first_range, "library": library, "library_mass": library_mass, "shuffle": shuffle}


def reference(queries, query_mass, first_range, library, library_mass, shuffle):
    epsilon = 1e-06
    lib_scale = lax.rsqrt(lax.optimization_barrier(jnp.sum(jnp.square(library.astype(jnp.float32)), axis=1)) + epsilon)
    decoy = jnp.take(library, shuffle, axis=1)
    row_index = jnp.arange(LIBRARY_ROWS, dtype=jnp.int32)
    lib_global = row_index // RANGE_ROWS * BINS + library_mass

    def one_block(inputs):
        block, offsets, range_start = inputs
        q_scale = lax.rsqrt(lax.optimization_barrier(jnp.sum(jnp.square(block.astype(jnp.float32)), axis=1)) + epsilon)
        first_row = (range_start * RANGE_ROWS).astype(jnp.int32)
        spectra = lax.dynamic_slice_in_dim(library, first_row, WINDOW * RANGE_ROWS, 0)
        shuffled = lax.dynamic_slice_in_dim(decoy, first_row, WINDOW * RANGE_ROWS, 0)
        scales = lax.dynamic_slice_in_dim(lib_scale, first_row, WINDOW * RANGE_ROWS, 0)
        masses = lax.dynamic_slice_in_dim(lib_global, first_row, WINDOW * RANGE_ROWS, 0)
        q_global = range_start * BINS + offsets
        allowed = jnp.abs(q_global[:, None] - masses[None, :]) <= TOLERANCE
        factor = q_scale[:, None] * scales[None, :]
        target_score = jnp.dot(block, spectra.T, preferred_element_type=jnp.float32) * factor
        decoy_score = jnp.dot(block, shuffled.T, preferred_element_type=jnp.float32) * factor
        target_score = jnp.where(allowed, target_score, -3.0)
        decoy_score = jnp.where(allowed, decoy_score, -3.0)
        target_top = lax.top_k(target_score, TOP_HITS)[0].T
        decoy_top = lax.top_k(decoy_score, TOP_HITS)[0].T
        return (target_top, decoy_top)
    target_best, decoy_best = lax.map(one_block, (queries, query_mass, first_range))
    return (target_best, decoy_best)
```

```python
import functools

import jax
import jax.numpy as jnp
from jax import lax
from jax.experimental import pallas as pl
from jax.experimental.pallas import tpu as pltpu
from jax.sharding import PartitionSpec as P

BINS = 16
TOLERANCE = 4
WINDOW = 3
TOP_HITS = 5
NZ, NX, NC, NY = 8, 4, 2, 4
CHIPS = NZ * NX
SLOTS = 4
ROWS = 8
LANES = 128
OFFSET = 64.0
epsilon = 1e-06
floor_score = -3.0
EMPTY = -1e30
MESH = pl.DeviceIdType.MESH
Z_ORDER = (4, 3, 5, 2, 6, 1, 7)


def insert(best, new, start=0):
    best = list(best)
    for k in range(start, TOP_HITS):
        high = jnp.maximum(best[k], new)
        if k + 1 < TOP_HITS:
            new = jnp.minimum(best[k], new)
        best[k] = high
    return best


def merged(former, latter):
    for k in range(TOP_HITS):
        former = insert(former, latter[k], k)
    return former


def swap_blocks(table):
    row = lax.broadcasted_iota(jnp.int32, table.shape, 0)
    segment = lax.broadcasted_iota(jnp.int32, table.shape, 1) // ROWS
    for bit in range(4):
        step = 1 << bit
        up = pltpu.roll(pltpu.roll(table, 16 - step, 0), ROWS * step, 1)
        down = pltpu.roll(pltpu.roll(table, step, 0), LANES - ROWS * step, 1)
        row_bit = (row // step) % 2
        segment_bit = (segment // step) % 2
        table = jnp.where(row_bit == segment_bit, table, jnp.where(row_bit == 0, up, down))
    return table


def search_kernel(
    first_ref, send, msg, lib, lib_mass, shuffle, q_scale, out,
    zbuf, qbuf, mbuf, lbuf, lmbuf, decoy, onehot, qsel, scale_rep, mass_rep,
    score_t, score_d, obuf, rbuf, abuf, fin, ybuf,
    z_send, z_recv, x_send, x_recv, m_send, m_recv, r_send, r_recv,
    l_send, l_recv, c_send, c_recv, lm_send, lm_recv, y_send, y_recv, here_sem,
):
    m = lax.axis_index("mass")
    y = lax.axis_index("sub")
    depth = lib.shape[1]
    lib_rows = lib.shape[0]
    range_rows = NY * lib_rows
    z = m // (NX * NC)
    x = (m // NC) % NX
    c = m % NC
    g = m // NC
    partner = m + 1 - 2 * c

    def device(chip):
        return (chip * NC + c, y)

    def turn(value, step, count):
        return lax.rem(value + step, count)

    barrier = pltpu.get_barrier_semaphore()

    def greet(k, carry):
        pl.semaphore_signal(barrier, inc=1, device_id=device(turn(g, k, CHIPS)), device_id_type=MESH)
        return carry

    lax.fori_loop(1, CHIPS, greet, 0)
    for step in range(1, NY):
        pl.semaphore_signal(barrier, inc=1, device_id=(m, turn(y, step, NY)), device_id_type=MESH)
    for step in range(NY):
        pl.semaphore_signal(barrier, inc=1, device_id=(partner, turn(y, step, NY)), device_id_type=MESH)
    pl.semaphore_wait(barrier, CHIPS - 1 + NY - 1 + NY)

    def remote(src, dst, send_sem, recv_sem, target):
        return pltpu.make_async_remote_copy(
            src_ref=src, dst_ref=dst, send_sem=send_sem, recv_sem=recv_sem,
            device_id=target, device_id_type=MESH,
        )

    def z_copy(dz):
        zt = turn(z, dz, NZ)
        return remote(
            send.at[pl.ds(zt * SLOTS, SLOTS)], zbuf.at[z], z_send.at[dz], z_recv.at[dz],
            device(zt * NX + x),
        )

    def pair_of(xt):
        return jnp.maximum(xt - 1, 0)

    def x_copy(dz, dx):
        zs = turn(z, NZ - dz, NZ)
        xt = turn(x, dx, NX)
        if dz == 0:
            src = send.at[pl.ds(z * SLOTS + pair_of(xt), 2)]
        else:
            src = zbuf.at[zs, pl.ds(pair_of(xt), 2)]
        if dx == 0:
            return pltpu.make_async_copy(src, qbuf.at[zs, x], here_sem.at[dz])
        return remote(
            src, qbuf.at[zs, x], x_send.at[dz, dx], x_recv.at[dz, dx], device(z * NX + xt)
        )

    for dz in Z_ORDER:
        z_copy(dz).start()
    for dx in (2, 1, 3, 0):
        x_copy(0, dx).start()

    half = lib_rows // 2
    up, down, opposite = turn(y, 1, NY), turn(y, NY - 1, NY), turn(y, 2, NY)
    own_keep = pltpu.make_async_copy(lib, lbuf.at[c, y], here_sem.at[NZ])
    own_up = remote(lib, lbuf.at[c, y], l_send.at[0], l_recv.at[0], (m, up))
    own_down = remote(lib, lbuf.at[c, y], l_send.at[1], l_recv.at[1], (m, down))
    own_core = remote(lib, lbuf.at[c, y], c_send.at[0], c_recv.at[0], (partner, y))
    own_up.start()
    own_down.start()
    own_core.start()
    own_keep.start()

    def mass_copy(k, carry):
        chip = turn(g, k, CHIPS)
        remote(msg.at[chip], mbuf.at[g], m_send, m_recv, device(chip)).start()
        return carry

    lax.fori_loop(1, CHIPS, mass_copy, 0)
    mass_keep = pltpu.make_async_copy(msg.at[g], mbuf.at[g], here_sem.at[NZ + 1])
    mass_keep.start()
    lm_keep = pltpu.make_async_copy(lib_mass, lmbuf.at[c, y], here_sem.at[NZ + 2])
    lm_keep.start()
    lm_copies = []
    for core in range(NC):
        for step in range(NY):
            if core == 0 and step == 0:
                continue
            at = core * NY + step
            lm_copies.append(remote(
                lib_mass, lmbuf.at[c, y], lm_send.at[at], lm_recv.at[at],
                (m if core == 0 else partner, turn(y, step, NY)),
            ))
    for copy in lm_copies:
        copy.start()

    chunk = 64
    names = shuffle[...]

    def build(i, carry):
        base = pl.multiple_of(i * chunk, chunk)
        index = lax.broadcasted_iota(jnp.int32, (chunk, depth), 0) + base
        onehot[pl.ds(base, chunk), :] = jnp.where(index == names, 1.0, 0.0).astype(jnp.bfloat16)
        return carry

    lax.fori_loop(0, depth // chunk, build, 0)

    for dz in Z_ORDER:
        z_copy(dz).wait_recv()
        for dx in (2, 1, 3, 0):
            x_copy(dz, dx).start()

    own_up.wait_recv()
    relay_up = remote(
        lbuf.at[c, down, pl.ds(0, half)], lbuf.at[c, down, pl.ds(0, half)],
        l_send.at[2], l_recv.at[2], (m, up),
    )
    relay_up.start()
    core_down = remote(lbuf.at[c, down], lbuf.at[c, down], c_send.at[1], c_recv.at[1], (partner, y))
    core_down.start()
    own_down.wait_recv()
    relay_down = remote(
        lbuf.at[c, up, pl.ds(half, half)], lbuf.at[c, up, pl.ds(half, half)],
        l_send.at[3], l_recv.at[3], (m, down),
    )
    relay_down.start()
    core_up = remote(lbuf.at[c, up], lbuf.at[c, up], c_send.at[2], c_recv.at[2], (partner, y))
    core_up.start()
    relay_up.wait_recv()
    relay_down.wait_recv()
    core_opposite = remote(
        lbuf.at[c, opposite], lbuf.at[c, opposite], c_send.at[3], c_recv.at[3], (partner, y)
    )
    core_opposite.start()

    own_keep.wait()
    lm_keep.wait()
    mass_keep.wait()
    for copy in lm_copies:
        copy.wait()
    for copy in (own_core, core_down, core_up, core_opposite):
        copy.wait()
    for copy in (own_up, own_down, relay_up, relay_down):
        copy.wait_send()
    for sem in (m_send, m_recv):
        pltpu.make_async_copy(msg.at[pl.ds(0, CHIPS - 1)], mbuf.at[pl.ds(0, CHIPS - 1)], sem).wait()

    def prepare(i, carry):
        e = i // NY
        piece = i % NY
        base = pl.multiple_of(piece * lib_rows, lib_rows)
        spectra = lbuf[e, piece]
        wide = spectra.astype(jnp.float32)
        total = jnp.sum(wide * wide, axis=1, keepdims=True)
        scale_rep[e, pl.ds(base, lib_rows), :] = jnp.broadcast_to(
            lax.rsqrt(total + epsilon), (lib_rows, LANES)
        )
        mass = jnp.broadcast_to(lmbuf[e, piece], (lib_rows, LANES)).T
        mass_rep[e, pl.ds(base, lib_rows), :] = mass + ((g * NC + e) * BINS).astype(jnp.float32)
        decoy[e, pl.ds(base, lib_rows), :] = jnp.dot(
            spectra, onehot[...], preferred_element_type=jnp.float32
        ).astype(jnp.bfloat16)
        return carry

    lax.fori_loop(0, NC * NY, prepare, 0)

    for dz in (0,) + Z_ORDER:
        for dx in range(NX):
            if dx:
                x_copy(dz, dx).wait()
            else:
                x_copy(dz, dx).wait()
        if dz:
            z_copy(dz).wait_send()

    row8 = lax.broadcasted_iota(jnp.int32, (ROWS, LANES), 0)
    for e in range(NC):
        def choose(i, carry):
            zs = i // 2
            xs = (i % 2) * 2
            codes = mbuf[pl.ds(i * 2, 2), e]
            code = jnp.max(codes, axis=-1, keepdims=True)
            odd = code - 2.0 * jnp.floor(code * 0.5)
            first = qbuf[zs, pl.ds(xs, 2), 0].astype(jnp.float32)
            second = qbuf[zs, pl.ds(xs, 2), 1].astype(jnp.float32)
            picked = jnp.where(odd > 0.5, second, first)
            base = pl.multiple_of(i * 16, 16)
            qsel[pl.ds(base, 16), :] = picked.reshape(2 * ROWS, depth).astype(jnp.bfloat16)
            return carry

        lax.fori_loop(0, CHIPS // 2, choose, 0)

        def score(i, carry):
            base = pl.multiple_of(i * lib_rows, lib_rows)
            block = qsel[...]
            score_t[pl.ds(base, lib_rows), :] = lax.dot_general(
                lbuf[e, i], block, (((1,), (1,)), ((), ())), preferred_element_type=jnp.float32
            )
            score_d[pl.ds(base, lib_rows), :] = lax.dot_general(
                decoy[e, pl.ds(base, lib_rows), :], block, (((1,), (1,)), ((), ())),
                preferred_element_type=jnp.float32,
            )
            return carry

        lax.fori_loop(0, NY, score, 0)

        for lg in range(2):
            codes = mbuf[pl.ds(lg * 16, 16), e]
            code = jnp.sum(codes, axis=0)
            q_mass = jnp.broadcast_to(jnp.floor(code * 0.5) - OFFSET, (ROWS, LANES))

            def scan(i, best):
                base = pl.multiple_of(i * ROWS, ROWS)
                scale = scale_rep[e, pl.ds(base, ROWS), :]
                mass = mass_rep[e, pl.ds(base, ROWS), :]
                allowed = jnp.abs(q_mass - mass) <= TOLERANCE
                target = score_t[pl.ds(base, ROWS), lg * LANES:(lg + 1) * LANES] * scale
                shuffled = score_d[pl.ds(base, ROWS), lg * LANES:(lg + 1) * LANES] * scale
                target = insert(best[:TOP_HITS], jnp.where(allowed, target, EMPTY))
                shuffled = insert(best[TOP_HITS:], jnp.where(allowed, shuffled, EMPTY))
                return tuple(target + shuffled)

            nothing = jnp.full((ROWS, LANES), EMPTY, jnp.float32)
            best = lax.fori_loop(
                0, range_rows // ROWS, scan, (nothing,) * (2 * TOP_HITS), unroll=4
            )
            lanes = []
            for part in (list(best[:TOP_HITS]), list(best[TOP_HITS:])):
                for shift in (4, 2, 1):
                    part = merged(part, [pltpu.roll(v, shift, 0) for v in part])
                lanes += part
            upper = lanes[0]
            for k in range(1, 8):
                upper = jnp.where(row8 == k, lanes[k], upper)
            lower = jnp.where(row8 == 0, lanes[8], lanes[9])
            table = swap_blocks(jnp.concatenate([upper, lower], axis=0))
            for k in range(16):
                obuf[lg * 16 + k, e] = table[k:k + 1, :]

    def result_copy(k, carry):
        chip = turn(g, k, CHIPS)
        remote(obuf.at[chip], rbuf.at[pl.ds(g * 2, 2)], r_send, r_recv, device(chip)).start()
        return carry

    lax.fori_loop(1, CHIPS, result_copy, 0)
    result_keep = pltpu.make_async_copy(obuf.at[g], rbuf.at[pl.ds(g * 2, 2)], here_sem.at[NZ + 3])
    result_keep.start()
    result_keep.wait()
    for sem in (r_send, r_recv):
        pltpu.make_async_copy(
            rbuf.at[pl.ds(0, 2 * (CHIPS - 1))], rbuf.at[pl.ds(0, 2 * (CHIPS - 1))], sem
        ).wait()

    blocks = q_scale.shape[0]
    for b in range(blocks):
        start = first_ref[b]
        for w in range(WINDOW):
            abuf[w, b:b + 1, :] = rbuf[start + w]
    best = None
    for w in range(WINDOW):
        rows = abuf[w]
        parts = [rows] + [pltpu.roll(rows, LANES - ROWS * k, 1) for k in range(1, TOP_HITS)]
        best = parts if best is None else merged(best, parts)
    segment = lax.broadcasted_iota(jnp.int32, (blocks, LANES), 1) // ROWS
    final = jnp.zeros((blocks, LANES), jnp.float32)
    for k in range(TOP_HITS):
        moved = pltpu.roll(best[k], ROWS * k, 1) if k else best[k]
        final = jnp.where((segment == k) | (segment == TOP_HITS + k), moved, final)
    final = jnp.where(final <= 0.5 * EMPTY, floor_score, final * q_scale[...])
    fin[...] = final
    copies = [
        remote(fin, ybuf.at[y], y_send.at[step], y_recv.at[step], (m, turn(y, step, NY)))
        for step in range(1, NY)
    ]
    for copy in copies:
        copy.start()
    own = pltpu.make_async_copy(fin, ybuf.at[y], here_sem.at[NZ + 4])
    own.start()
    own.wait()
    for copy in copies:
        copy.wait()
    out[...] = ybuf[...]


def per_device(queries, query_mass, first_range, library, library_mass, shuffle):
    m = lax.axis_index("mass")
    y = lax.axis_index("sub")
    count, q_rows, depth = queries.shape
    lib_rows = library.shape[0]
    quarters = queries.reshape(count * NY, ROWS, depth)
    rows_z = jnp.arange(NZ, dtype=jnp.int32)[:, None, None] * (NX * NC)
    low = rows_z - 2 + 3 * jnp.arange(SLOTS, dtype=jnp.int32)[None, :, None]
    inside = (first_range >= low) & (first_range <= low + 2) & (first_range <= rows_z + 7)
    block_ids = jnp.arange(count, dtype=jnp.int32)
    chosen = jnp.sum(jnp.where(inside, block_ids, 0), axis=2).reshape(-1)
    send = jnp.take(quarters, chosen * NY + y, axis=0, mode="clip")

    own_mass = lax.dynamic_slice(query_mass, (0, y * ROWS), (count, ROWS))
    own_global = own_mass + first_range[:, None] * BINS
    ranges = jnp.arange(CHIPS * NC, dtype=jnp.int32)[:, None]
    covers = (first_range[None, :] <= ranges) & (ranges < first_range[None, :] + WINDOW)
    row_start = (ranges // 8) * 8
    pair = jnp.maximum((ranges % 8) // 2 - 1, 0)
    flag = (first_range[None, :] - row_start + 2) // 3 - pair
    code = (own_global[None, :, :] + int(OFFSET)) * 2 + flag[:, :, None]
    code = jnp.sum(jnp.where(covers[:, :, None], code, 0), axis=1).astype(jnp.float32)
    lane = jnp.arange(LANES, dtype=jnp.int32)
    msg = jnp.where(lane // ROWS == (m // NC) % 16, jnp.tile(code, (1, LANES // ROWS)), 0.0)
    msg = msg.reshape(CHIPS, NC, 1, LANES)

    own_rows = lax.dynamic_slice(queries, (0, y * ROWS, 0), (count, ROWS, depth)).astype(jnp.float32)
    q_scale = lax.rsqrt(jnp.sum(own_rows * own_rows, axis=2) + epsilon)
    q_scale = jnp.tile(q_scale, (1, LANES // ROWS))

    vmem = pl.BlockSpec(memory_space=pltpu.VMEM)
    f32, bf16 = jnp.float32, jnp.bfloat16
    dma = pltpu.SemaphoreType.DMA
    range_rows = NY * lib_rows
    found = pl.pallas_call(
        search_kernel,
        out_shape=jax.ShapeDtypeStruct((NY, count, LANES), f32),
        in_specs=[pl.BlockSpec(memory_space=pltpu.SMEM)] + [vmem] * 6,
        out_specs=vmem,
        scratch_shapes=[
            pltpu.VMEM((NZ, SLOTS, ROWS, depth), bf16),
            pltpu.VMEM((NZ, NX, 2, ROWS, depth), bf16),
            pltpu.VMEM((CHIPS, NC, 1, LANES), f32),
            pltpu.VMEM((NC, NY, lib_rows, depth), bf16),
            pltpu.VMEM((NC, NY, 1, LANES), f32),
            pltpu.VMEM((NC, range_rows, depth), bf16),
            pltpu.VMEM((depth, depth), bf16),
            pltpu.VMEM((CHIPS * ROWS, depth), bf16),
            pltpu.VMEM((NC, range_rows, LANES), f32),
            pltpu.VMEM((NC, range_rows, LANES), f32),
            pltpu.VMEM((range_rows, CHIPS * ROWS), f32),
            pltpu.VMEM((range_rows, CHIPS * ROWS), f32),
            pltpu.VMEM((CHIPS, NC, 1, LANES), f32),
            pltpu.VMEM((CHIPS * NC, 1, LANES), f32),
            pltpu.VMEM((WINDOW, count, LANES), f32),
            pltpu.VMEM((count, LANES), f32),
            pltpu.VMEM((NY, count, LANES), f32),
            dma((NZ,)), dma((NZ,)), dma((NZ, NX)), dma((NZ, NX)), dma, dma, dma, dma,
            dma((4,)), dma((4,)), dma((4,)), dma((4,)), dma((8,)), dma((8,)), dma((NY,)), dma((NY,)),
            dma((NZ + 5,)),
        ],
        compiler_params=pltpu.CompilerParams(collective_id=0, has_side_effects=True),
        name="search",
    )(
        first_range, send, msg, library, library_mass.astype(f32).reshape(1, LANES),
        shuffle.reshape(1, depth), q_scale,
    )
    found = found.reshape(NY, count, 16, ROWS)[:, :, :2 * TOP_HITS]
    found = jnp.transpose(found, (1, 2, 0, 3)).reshape(count, 2 * TOP_HITS, q_rows)
    return (found[:, :TOP_HITS], found[:, TOP_HITS:])


def solution(mesh):
    return jax.shard_map(
        per_device,
        mesh=mesh,
        in_specs=(
            P("mass", None, None),
            P("mass", None),
            P("mass"),
            P(("mass", "sub"), None),
            P(("mass", "sub")),
            P(),
        ),
        out_specs=(P("mass", None, None), P("mass", None, None)),
        check_vma=False,
    )
```

```python
import jax
import jax.numpy as jnp
from jax import lax
from jax.experimental import pallas as pl
from jax.experimental.pallas import tpu as pltpu
from jax.sharding import PartitionSpec as P

BINS = 16
TOLERANCE = 4
WINDOW = 3
TOP_HITS = 5
NZ, NX, NC, NY = 8, 4, 2, 4
CHIPS = NZ * NX
SLOTS = 4
ROWS = 8
LANES = 128
OFFSET = 64.0
epsilon = 1e-06
floor_score = -3.0
EMPTY = -1e30
MESH = pl.DeviceIdType.MESH
ORDER = (0, 1, 7, 2, 6, 3, 5, 4)


def insert(best, new, start=0):
    best = list(best)
    for k in range(start, TOP_HITS):
        high = jnp.maximum(best[k], new)
        if k + 1 < TOP_HITS:
            new = jnp.minimum(best[k], new)
        best[k] = high
    return best


def merged(former, latter):
    for k in range(TOP_HITS):
        former = insert(former, latter[k], k)
    return former


def spread(rows):
    for shift in (8, 16, 32, 64):
        rows = rows + pltpu.roll(rows, shift, 1)
    return rows


def swap_blocks(table):
    row = lax.broadcasted_iota(jnp.int32, table.shape, 0)
    segment = lax.broadcasted_iota(jnp.int32, table.shape, 1) // ROWS
    for bit in range(4):
        step = 1 << bit
        up = pltpu.roll(pltpu.roll(table, 16 - step, 0), ROWS * step, 1)
        down = pltpu.roll(pltpu.roll(table, step, 0), LANES - ROWS * step, 1)
        row_bit = (row // step) % 2
        segment_bit = (segment // step) % 2
        table = jnp.where(row_bit == segment_bit, table, jnp.where(row_bit == 0, up, down))
    return table


def search_kernel(
    first_ref, queries, q_mass, lib, lib_mass, shuffle, out,
    qown, send, code, zbuf, zcode, qbuf, xcode, lmbuf, spectra, onehot, qsel, scale_rep, mass_rep,
    flags, scores, obuf, rbuf, abuf, norms, fin, ybuf,
    z_send, z_recv, zc_send, zc_recv, x_send, x_recv, xc_send, xc_recv, r_send, r_recv,
    l_send, l_recv, c_send, c_recv, lm_send, lm_recv, y_send, y_recv, here_sem,
):
    m = lax.axis_index("mass")
    y = lax.axis_index("sub")
    blocks = q_mass.shape[0]
    lib_rows, depth = lib.shape
    range_rows = NY * lib_rows
    z = m // (NX * NC)
    x = (m // NC) % NX
    c = m % NC
    g = m // NC
    partner = m + 1 - 2 * c

    def device(chip):
        return (chip * NC + c, y)

    def turn(value, step, count):
        return lax.rem(value + step, count)

    def remote(src, dst, send_sem, recv_sem, target):
        return pltpu.make_async_remote_copy(
            src_ref=src, dst_ref=dst, send_sem=send_sem, recv_sem=recv_sem,
            device_id=target, device_id_type=MESH,
        )

    barrier = pltpu.get_barrier_semaphore()
    peers = [device(turn(z, s, NZ) * NX + x) for s in range(1, NZ)]
    peers += [device(z * NX + turn(x, s, NX)) for s in range(1, NX)]
    peers += [(m, turn(y, s, NY)) for s in range(1, NY)]
    peers += [(partner, turn(y, s, NY)) for s in range(NY)]
    for peer in peers:
        pl.semaphore_signal(barrier, inc=1, device_id=peer, device_id_type=MESH)

    take_queries = pltpu.make_async_copy(queries.at[:, y], qown, here_sem.at[0])
    take_queries.start()
    own_lib = spectra.at[c, 0, pl.ds(y * lib_rows, lib_rows)]
    take_lib = pltpu.make_async_copy(lib, own_lib, here_sem.at[1])
    take_lib.start()
    take_mass = pltpu.make_async_copy(lib_mass, lmbuf.at[c, y], here_sem.at[2])
    take_mass.start()

    lane = lax.broadcasted_iota(jnp.int32, (ROWS, LANES), 1)
    row8 = lax.broadcasted_iota(jnp.int32, (ROWS, LANES), 0)
    wide_lane = lax.broadcasted_iota(jnp.int32, (blocks, LANES), 1)
    own_mass = jnp.concatenate(
        [q_mass[...].astype(jnp.float32), jnp.zeros((blocks, LANES - NY * ROWS), jnp.float32)], axis=1
    )
    own_mass = pltpu.roll(own_mass, turn(LANES - y * ROWS, 0, LANES), 1)
    own_mass = spread(jnp.where(wide_lane < ROWS, own_mass, 0.0))
    pair_start = jnp.maximum(row8 // 2 - 1, 0)
    for at, dz in enumerate(ORDER):
        base = turn(z, dz, NZ) * (NX * NC)
        ranges = row8 + base
        threshold = base + 3 * pair_start + 1
        tile = jnp.zeros((ROWS, LANES), jnp.float32)
        for b in range(blocks):
            start = first_ref[b]
            shift = ((start - base) * BINS).astype(jnp.float32) + OFFSET
            value = own_mass[b:b + 1, :] + shift
            value = jnp.where(start >= threshold, -value, value)
            ahead = ranges - start
            tile = jnp.where((ahead >= 0) & (ahead < WINDOW), value, tile)
        dx = lax.rem(row8 // 2 - x + NX, NX)
        place = lax.rem(at * NX + dx, 16)
        code[at] = jnp.where(lane // ROWS == place, tile, 0.0).astype(jnp.bfloat16)

    take_queries.wait()

    def gather(i, carry):
        row = i // SLOTS
        low = row * (NX * NC) - 2 + 3 * (i % SLOTS)
        high = jnp.minimum(low + 2, row * (NX * NC) + NX * NC - 1)
        chosen = jnp.int32(0)
        for b in range(blocks):
            start = first_ref[b]
            chosen = jnp.where((start >= low) & (start <= high), b, chosen)
        send[i] = qown[chosen]
        return carry

    lax.fori_loop(0, NZ * SLOTS, gather, 0)
    take_lib.wait()
    take_mass.wait()

    pl.semaphore_wait(barrier, len(peers))

    def z_copies(at):
        zt = turn(z, ORDER[at], NZ)
        target = device(zt * NX + x)
        return (
            remote(send.at[pl.ds(zt * SLOTS, SLOTS)], zbuf.at[at], z_send.at[at], z_recv.at[at], target),
            remote(code.at[at], zcode.at[at], zc_send.at[at], zc_recv.at[at], target),
        )

    def x_copies(at, dx):
        xt = turn(x, dx, NX)
        start = jnp.maximum(xt - 1, 0)
        if at:
            pair, codes = zbuf.at[at, pl.ds(start, 2)], zcode.at[at]
        else:
            pair, codes = send.at[pl.ds(z * SLOTS + start, 2)], code.at[0]
        to_pair, to_codes = qbuf.at[at, dx], xcode.at[at, dx]
        if dx == 0:
            return (
                pltpu.make_async_copy(pair, to_pair, here_sem.at[3 + at]),
                pltpu.make_async_copy(codes, to_codes, here_sem.at[3 + NZ + at]),
            )
        target = device(z * NX + xt)
        return (
            remote(pair, to_pair, x_send.at[at, dx], x_recv.at[at, dx], target),
            remote(codes, to_codes, xc_send.at[at, dx], xc_recv.at[at, dx], target),
        )

    def start(copies):
        for copy in copies:
            copy.start()

    def forward(at):
        for dx in (2, 1, 3, 0):
            start(x_copies(at, dx))

    for at in range(1, NZ):
        start(z_copies(at))
    forward(0)

    half = lib_rows // 2
    up, down, opposite = turn(y, 1, NY), turn(y, NY - 1, NY), turn(y, 2, NY)

    def piece(at, first=0, count=lib_rows):
        return spectra.at[c, 0, pl.ds(at * lib_rows + first, count)]

    def piece_copy(part, sems, at, target):
        return remote(part, part, sems[0].at[at], sems[1].at[at], target)

    l_sems, c_sems = (l_send, l_recv), (c_send, c_recv)
    own_up = piece_copy(piece(y), l_sems, 0, (m, up))
    own_down = piece_copy(piece(y), l_sems, 1, (m, down))
    own_core = piece_copy(piece(y), c_sems, 0, (partner, y))
    start((own_up, own_down, own_core))
    lm_copies = []
    for core in range(NC):
        for step in range(NY):
            if core or step:
                at = core * NY + step
                target = (partner if core else m, turn(y, step, NY))
                lm_copies.append(remote(
                    lmbuf.at[c, y], lmbuf.at[c, y], lm_send.at[at], lm_recv.at[at], target
                ))
    start(lm_copies)

    chunk = 64
    names = shuffle[...]

    def build(i, carry):
        base = pl.multiple_of(i * chunk, chunk)
        index = lax.broadcasted_iota(jnp.int32, (chunk, depth), 0) + base
        onehot[pl.ds(base, chunk), :] = jnp.where(index == names, 1.0, 0.0).astype(jnp.bfloat16)
        return carry

    lax.fori_loop(0, depth // chunk, build, 0)

    def prepare(e, at):
        base = pl.multiple_of(at * lib_rows, lib_rows)
        rows = spectra[e, 0, pl.ds(base, lib_rows), :]
        wide = rows.astype(jnp.float32)
        total = jnp.sum(wide * wide, axis=1, keepdims=True)
        scale_rep[e, pl.ds(base, lib_rows), :] = jnp.broadcast_to(
            lax.rsqrt(total + epsilon), (lib_rows, LANES)
        )
        spectra[e, 1, pl.ds(base, lib_rows), :] = jnp.dot(
            rows, onehot[...], preferred_element_type=jnp.float32
        ).astype(jnp.bfloat16)

    def arrive(at):
        for copy in z_copies(at):
            copy.wait_recv()
        forward(at)

    arrive(1)
    arrive(2)
    prepare(c, y)
    arrive(3)
    arrive(4)

    def norm(i, carry):
        wide = qown[pl.ds(i * 2, 2)].astype(jnp.float32).reshape(2 * ROWS, depth)
        total = jnp.sum(wide * wide, axis=1, keepdims=True)
        norms[pl.ds(pl.multiple_of(i * 16, 16), 16), :] = jnp.broadcast_to(
            lax.rsqrt(total + epsilon), (2 * ROWS, LANES)
        )
        return carry

    lax.fori_loop(0, blocks // 2, norm, 0)

    own_up.wait_recv()
    relay_up = piece_copy(piece(down, 0, half), l_sems, 2, (m, up))
    core_down = piece_copy(piece(down), c_sems, 1, (partner, y))
    start((relay_up, core_down))
    own_down.wait_recv()
    relay_down = piece_copy(piece(up, half, half), l_sems, 3, (m, down))
    core_up = piece_copy(piece(up), c_sems, 2, (partner, y))
    start((relay_down, core_up))
    arrive(5)
    own_core.wait_recv()
    prepare(1 - c, y)
    prepare(c, down)
    arrive(6)
    prepare(c, up)
    core_down.wait_recv()
    prepare(1 - c, down)
    arrive(7)
    core_up.wait_recv()
    prepare(1 - c, up)
    relay_up.wait_recv()
    relay_down.wait_recv()
    core_opposite = piece_copy(piece(opposite), c_sems, 3, (partner, y))
    core_opposite.start()
    prepare(c, opposite)

    for copy in lm_copies:
        copy.wait()
    for e in range(NC):
        for at in range(NY):
            mass = jnp.broadcast_to(lmbuf[e, at].astype(jnp.float32), (lib_rows, LANES)).T
            mass = mass + ((x * NC + e) * BINS).astype(jnp.float32) + OFFSET
            mass_rep[e, at * lib_rows:(at + 1) * lib_rows, :] = mass
    core_opposite.wait_recv()
    prepare(1 - c, opposite)

    tables = [[None, None], [None, None]]
    for lg in range(2):
        first_at = lg * NZ // 2
        combined = jnp.zeros((ROWS, LANES), jnp.float32)
        for at in range(first_at, first_at + NZ // 2):
            for dx in range(NX):
                for copy in x_copies(at, dx):
                    if dx:
                        copy.wait_recv()
                    else:
                        copy.wait()
                tile = xcode[at, dx].astype(jnp.float32)
                combined = combined + jnp.abs(tile)
                flags[at * NX + dx] = jnp.broadcast_to(
                    jnp.sum(tile, axis=1, keepdims=True), (ROWS, LANES)
                )

        def choose(i, carry):
            at = first_at + i // 2
            side = (i % 2) * 2
            first = qbuf[at, pl.ds(side, 2), 0].astype(jnp.float32)
            second = qbuf[at, pl.ds(side, 2), 1].astype(jnp.float32)
            base = pl.multiple_of(i * 16, 16)
            for e in range(NC):
                flag = flags[pl.ds(at * NX + side, 2), pl.ds(x * NC + e, 1), :][:, :, :1]
                picked = jnp.where(flag < 0.0, second, first)
                qsel[e, pl.ds(base, 16), :] = picked.reshape(2 * ROWS, depth).astype(jnp.bfloat16)
            return carry

        lax.fori_loop(0, NZ, choose, 0)

        masses = []
        for e in range(NC):
            scores[e] = lax.dot_general(
                spectra[e].reshape(2 * range_rows, depth), qsel[e], (((1,), (1,)), ((), ())),
                preferred_element_type=jnp.float32,
            )
            code_row = jnp.sum(jnp.where(row8 == x * NC + e, combined, 0.0), axis=0, keepdims=True)
            masses.append(jnp.broadcast_to(code_row, (ROWS, LANES)))

        def scan(i, best):
            base = pl.multiple_of(i * ROWS, ROWS)
            found = []
            for e in range(NC):
                scale = scale_rep[e, pl.ds(base, ROWS), :]
                allowed = jnp.abs(masses[e] - mass_rep[e, pl.ds(base, ROWS), :]) <= TOLERANCE
                for kind in range(2):
                    score = scores[e, pl.ds(kind * range_rows + base, ROWS), :] * scale
                    at = (e * 2 + kind) * TOP_HITS
                    found += insert(best[at:at + TOP_HITS], jnp.where(allowed, score, EMPTY))
            return tuple(found)

        nothing = jnp.full((ROWS, LANES), EMPTY, jnp.float32)
        best = lax.fori_loop(
            0, range_rows // ROWS, scan, (nothing,) * (4 * TOP_HITS), unroll=2
        )
        for e in range(NC):
            lanes = []
            for kind in range(2):
                at = (e * 2 + kind) * TOP_HITS
                part = list(best[at:at + TOP_HITS])
                for shift in (4, 2, 1):
                    part = merged(part, [pltpu.roll(v, shift, 0) for v in part])
                lanes += part
            upper = lanes[0]
            for k in range(1, 8):
                upper = jnp.where(row8 == k, lanes[k], upper)
            lower = jnp.where(row8 == 0, lanes[8], lanes[9])
            table = swap_blocks(jnp.concatenate([upper, lower], axis=0))
            for k in range(16):
                obuf[lg * 16 + k, e] = table[k:k + 1, :]

    for at in range(NZ):
        for dx in range(NX):
            if at or dx:
                chip = turn(z, NZ - ORDER[at], NZ) * NX + turn(x, NX - dx, NX)
                remote(
                    obuf.at[at * NX + dx], rbuf.at[pl.ds(g * NC, NC)], r_send, r_recv, device(chip)
                ).start()
    keep = pltpu.make_async_copy(obuf.at[0], rbuf.at[pl.ds(g * NC, NC)], here_sem.at[0])
    keep.start()

    for at in range(NZ):
        if at:
            for copy in z_copies(at):
                copy.wait_send()
        for dx in range(1, NX):
            for copy in x_copies(at, dx):
                copy.wait_send()
    for copy in (own_up, own_down, relay_up, relay_down, own_core, core_down, core_up, core_opposite):
        copy.wait_send()

    block_row = lax.broadcasted_iota(jnp.int32, (blocks, LANES), 0)
    q_scale = spread(jnp.where(wide_lane // ROWS == block_row, norms[...].T[:blocks], 0.0))

    keep.wait()
    for sem in (r_send, r_recv):
        others = rbuf.at[pl.ds(0, NC * (CHIPS - 1))]
        pltpu.make_async_copy(others, others, sem).wait()

    for b in range(blocks):
        first = first_ref[b]
        for w in range(WINDOW):
            abuf[w, b:b + 1, :] = rbuf[first + w]
    best = None
    for w in range(WINDOW):
        rows = abuf[w]
        parts = [rows] + [pltpu.roll(rows, LANES - ROWS * k, 1) for k in range(1, TOP_HITS)]
        best = parts if best is None else merged(best, parts)
    segment = wide_lane // ROWS
    final = jnp.zeros((blocks, LANES), jnp.float32)
    for k in range(TOP_HITS):
        moved = pltpu.roll(best[k], ROWS * k, 1) if k else best[k]
        final = jnp.where((segment == k) | (segment == TOP_HITS + k), moved, final)
    fin[...] = jnp.where(final <= 0.5 * EMPTY, floor_score, final * q_scale)
    copies = [
        remote(fin, ybuf.at[y], y_send.at[step], y_recv.at[step], (m, turn(y, step, NY)))
        for step in range(1, NY)
    ]
    start(copies)
    own = pltpu.make_async_copy(fin, ybuf.at[y], here_sem.at[1])
    own.start()
    own.wait()
    for copy in copies:
        copy.wait()
    out[...] = ybuf[...]


def per_device(queries, query_mass, first_range, library, library_mass, shuffle):
    count, q_rows, depth = queries.shape
    lib_rows = library.shape[0]
    f32, bf16 = jnp.float32, jnp.bfloat16
    vmem = pl.BlockSpec(memory_space=pltpu.VMEM)
    smem = pl.BlockSpec(memory_space=pltpu.SMEM)
    hbm = pl.BlockSpec(memory_space=pl.ANY)
    dma = pltpu.SemaphoreType.DMA
    range_rows = NY * lib_rows
    found = pl.pallas_call(
        search_kernel,
        out_shape=jax.ShapeDtypeStruct((NY, count, LANES), f32),
        in_specs=[smem, hbm, vmem, hbm, hbm, vmem],
        out_specs=vmem,
        scratch_shapes=[
            pltpu.VMEM((count, ROWS, depth), bf16),
            pltpu.VMEM((NZ * SLOTS, ROWS, depth), bf16),
            pltpu.VMEM((NZ, ROWS, LANES), bf16),
            pltpu.VMEM((NZ, SLOTS, ROWS, depth), bf16),
            pltpu.VMEM((NZ, ROWS, LANES), bf16),
            pltpu.VMEM((NZ, NX, 2, ROWS, depth), bf16),
            pltpu.VMEM((NZ, NX, ROWS, LANES), bf16),
            pltpu.VMEM((NC, NY, 1, LANES), jnp.int32),
            pltpu.VMEM((NC, 2, range_rows, depth), bf16),
            pltpu.VMEM((depth, depth), bf16),
            pltpu.VMEM((NC, LANES, depth), bf16),
            pltpu.VMEM((NC, range_rows, LANES), f32),
            pltpu.VMEM((NC, range_rows, LANES), f32),
            pltpu.VMEM((CHIPS, ROWS, LANES), f32),
            pltpu.VMEM((NC, 2 * range_rows, LANES), f32),
            pltpu.VMEM((CHIPS, NC, 1, LANES), f32),
            pltpu.VMEM((CHIPS * NC, 1, LANES), f32),
            pltpu.VMEM((WINDOW, count, LANES), f32),
            pltpu.VMEM((count * ROWS, LANES), f32),
            pltpu.VMEM((count, LANES), f32),
            pltpu.VMEM((NY, count, LANES), f32),
            dma((NZ,)), dma((NZ,)), dma((NZ,)), dma((NZ,)),
            dma((NZ, NX)), dma((NZ, NX)), dma((NZ, NX)), dma((NZ, NX)), dma, dma,
            dma((4,)), dma((4,)), dma((4,)), dma((4,)), dma((8,)), dma((8,)), dma((NY,)), dma((NY,)),
            dma((3 + 2 * NZ,)),
        ],
        compiler_params=pltpu.CompilerParams(collective_id=0, has_side_effects=True),
        name="search",
    )(
        first_range, queries.reshape(count, NY, ROWS, depth), query_mass, library,
        library_mass.reshape(1, LANES), shuffle.reshape(1, depth),
    )
    found = found.reshape(NY, count, 16, ROWS)[:, :, :2 * TOP_HITS]
    found = jnp.transpose(found, (1, 2, 0, 3)).reshape(count, 2 * TOP_HITS, q_rows)
    return (found[:, :TOP_HITS], found[:, TOP_HITS:])


def solution(mesh):
    return jax.shard_map(
        per_device,
        mesh=mesh,
        in_specs=(
            P("mass", None, None),
            P("mass", None),
            P("mass"),
            P(("mass", "sub"), None),
            P(("mass", "sub")),
            P(),
        ),
        out_specs=(P("mass", None, None), P("mass", None, None)),
        check_vma=False,
    )
```

```python
import jax
import jax.numpy as jnp
from jax import lax
from jax.experimental import pallas as pl
from jax.experimental.pallas import tpu as pltpu
from jax.sharding import PartitionSpec as P

BINS = 16
TOLERANCE = 4
WINDOW = 3
TOP_HITS = 5
NZ, NX, NC, NY = 8, 4, 2, 4
CHIPS = NZ * NX
SLOTS = 4
ROWS = 8
LANES = 128
OFFSET = 64.0
epsilon = 1e-06
floor_score = -3.0
EMPTY = -1e30
MESH = pl.DeviceIdType.MESH
ORDER = (0, 1, 7, 2, 6, 3, 5, 4)


def insert(best, new, start=0):
    best = list(best)
    for k in range(start, TOP_HITS):
        high = jnp.maximum(best[k], new)
        if k + 1 < TOP_HITS:
            new = jnp.minimum(best[k], new)
        best[k] = high
    return best


def merged(former, latter):
    for k in range(TOP_HITS):
        former = insert(former, latter[k], k)
    return former


def spread(rows):
    for shift in (8, 16, 32, 64):
        rows = rows + pltpu.roll(rows, shift, 1)
    return rows


def swap_blocks(table):
    row = lax.broadcasted_iota(jnp.int32, table.shape, 0)
    segment = lax.broadcasted_iota(jnp.int32, table.shape, 1) // ROWS
    for bit in range(4):
        step = 1 << bit
        up = pltpu.roll(pltpu.roll(table, 16 - step, 0), ROWS * step, 1)
        down = pltpu.roll(pltpu.roll(table, step, 0), LANES - ROWS * step, 1)
        row_bit = (row // step) % 2
        segment_bit = (segment // step) % 2
        table = jnp.where(row_bit == segment_bit, table, jnp.where(row_bit == 0, up, down))
    return table


def search_kernel(
    first_ref, queries, q_mass, lib, lib_mass, shuffle, out_t, out_d,
    qall, send, code, zbuf, zcode, qbuf, xcode, lmbuf, spectra, onehot, columns, scale_rep, mass_rep,
    scores, obuf, rbuf, abuf, norms, q_scale,
    z_send, z_recv, zc_send, zc_recv, x_send, x_recv, xc_send, xc_recv, r_send, r_recv,
    l_send, l_recv, c_send, c_recv, lm_send, lm_recv, here_sem,
):
    m = lax.axis_index("mass")
    y = lax.axis_index("sub")
    blocks = q_mass.shape[0]
    lib_rows, depth = lib.shape
    range_rows = NY * lib_rows
    z = m // (NX * NC)
    x = (m // NC) % NX
    c = m % NC
    g = m // NC
    partner = m + 1 - 2 * c

    def device(chip):
        return (chip * NC + c, y)

    def turn(value, step, count):
        return lax.rem(value + step, count)

    def remote(src, dst, send_sem, recv_sem, target):
        return pltpu.make_async_remote_copy(
            src_ref=src, dst_ref=dst, send_sem=send_sem, recv_sem=recv_sem,
            device_id=target, device_id_type=MESH,
        )

    barrier = pltpu.get_barrier_semaphore()
    peers = [device(turn(z, s, NZ) * NX + x) for s in range(1, NZ)]
    peers += [device(z * NX + turn(x, s, NX)) for s in range(1, NX)]
    peers += [(m, turn(y, s, NY)) for s in range(1, NY)]
    peers += [(partner, turn(y, s, NY)) for s in range(NY)]
    for peer in peers:
        pl.semaphore_signal(barrier, inc=1, device_id=peer, device_id_type=MESH)

    take_queries = pltpu.make_async_copy(queries, qall, here_sem.at[0])
    take_queries.start()
    own_lib = spectra.at[c, 0, pl.ds(y * lib_rows, lib_rows)]
    take_lib = pltpu.make_async_copy(lib, own_lib, here_sem.at[1])
    take_lib.start()
    take_mass = pltpu.make_async_copy(lib_mass, lmbuf.at[c, y], here_sem.at[2])
    take_mass.start()

    lane = lax.broadcasted_iota(jnp.int32, (ROWS, LANES), 1)
    row8 = lax.broadcasted_iota(jnp.int32, (ROWS, LANES), 0)
    wide_lane = lax.broadcasted_iota(jnp.int32, (blocks, LANES), 1)
    own_mass = jnp.concatenate(
        [q_mass[...].astype(jnp.float32), jnp.zeros((blocks, LANES - NY * ROWS), jnp.float32)], axis=1
    )
    own_mass = pltpu.roll(own_mass, turn(LANES - y * ROWS, 0, LANES), 1)
    own_mass = spread(jnp.where(wide_lane < ROWS, own_mass, 0.0))
    pair_start = jnp.maximum(row8 // 2 - 1, 0)
    for at, dz in enumerate(ORDER):
        base = turn(z, dz, NZ) * (NX * NC)
        ranges = row8 + base
        threshold = base + 3 * pair_start + 1
        tile = jnp.zeros((ROWS, LANES), jnp.float32)
        for b in range(blocks):
            start = first_ref[b]
            shift = ((start - base) * BINS).astype(jnp.float32) + OFFSET
            value = own_mass[b:b + 1, :] + shift
            value = jnp.where(start >= threshold, -value, value)
            ahead = ranges - start
            tile = jnp.where((ahead >= 0) & (ahead < WINDOW), value, tile)
        dx = lax.rem(row8 // 2 - x + NX, NX)
        place = lax.rem(at * NX + dx, 16)
        code[at] = jnp.where(lane // ROWS == place, tile, 0.0).astype(jnp.bfloat16)

    take_queries.wait()

    def gather(i, carry):
        row = i // SLOTS
        low = row * (NX * NC) - 2 + 3 * (i % SLOTS)
        high = jnp.minimum(low + 2, row * (NX * NC) + NX * NC - 1)
        chosen = jnp.int32(0)
        for b in range(blocks):
            start = first_ref[b]
            chosen = jnp.where((start >= low) & (start <= high), b, chosen)
        send[i] = qall[chosen, y]
        return carry

    lax.fori_loop(0, NZ * SLOTS, gather, 0)
    take_lib.wait()
    take_mass.wait()

    pl.semaphore_wait(barrier, len(peers))

    def z_copies(at):
        zt = turn(z, ORDER[at], NZ)
        target = device(zt * NX + x)
        return (
            remote(send.at[pl.ds(zt * SLOTS, SLOTS)], zbuf.at[at], z_send.at[at], z_recv.at[at], target),
            remote(code.at[at], zcode.at[at], zc_send.at[at], zc_recv.at[at], target),
        )

    def x_copies(at, dx):
        xt = turn(x, dx, NX)
        start = jnp.maximum(xt - 1, 0)
        if at:
            pair, codes = zbuf.at[at, pl.ds(start, 2)], zcode.at[at]
        else:
            pair, codes = send.at[pl.ds(z * SLOTS + start, 2)], code.at[0]
        to_pair, to_codes = qbuf.at[at, dx], xcode.at[at, dx]
        if dx == 0:
            return (
                pltpu.make_async_copy(pair, to_pair, here_sem.at[3 + at]),
                pltpu.make_async_copy(codes, to_codes, here_sem.at[3 + NZ + at]),
            )
        target = device(z * NX + xt)
        return (
            remote(pair, to_pair, x_send.at[at, dx], x_recv.at[at, dx], target),
            remote(codes, to_codes, xc_send.at[at, dx], xc_recv.at[at, dx], target),
        )

    def start(copies):
        for copy in copies:
            copy.start()

    def forward(at):
        for dx in (2, 1, 3, 0):
            start(x_copies(at, dx))

    for at in range(1, NZ):
        start(z_copies(at))
    forward(0)

    half = lib_rows // 2
    up, down, opposite = turn(y, 1, NY), turn(y, NY - 1, NY), turn(y, 2, NY)

    def piece(at, first=0, count=lib_rows):
        return spectra.at[c, 0, pl.ds(at * lib_rows + first, count)]

    def piece_copy(part, sems, at, target):
        return remote(part, part, sems[0].at[at], sems[1].at[at], target)

    l_sems, c_sems = (l_send, l_recv), (c_send, c_recv)
    own_up = piece_copy(piece(y), l_sems, 0, (m, up))
    own_down = piece_copy(piece(y), l_sems, 1, (m, down))
    own_core = piece_copy(piece(y), c_sems, 0, (partner, y))
    start((own_up, own_down, own_core))
    lm_copies = []
    for core in range(NC):
        for step in range(NY):
            if core or step:
                at = core * NY + step
                target = (partner if core else m, turn(y, step, NY))
                lm_copies.append(remote(
                    lmbuf.at[c, y], lmbuf.at[c, y], lm_send.at[at], lm_recv.at[at], target
                ))
    start(lm_copies)

    chunk = 64
    names = shuffle[...]

    def build(i, carry):
        base = pl.multiple_of(i * chunk, chunk)
        index = lax.broadcasted_iota(jnp.int32, (chunk, depth), 0) + base
        onehot[pl.ds(base, chunk), :] = jnp.where(index == names, 1.0, 0.0).astype(jnp.bfloat16)
        return carry

    lax.fori_loop(0, depth // chunk, build, 0)

    def prepare(e, at):
        base = pl.multiple_of(at * lib_rows, lib_rows)
        rows = spectra[e, 0, pl.ds(base, lib_rows), :]
        wide = rows.astype(jnp.float32)
        total = jnp.sum(wide * wide, axis=1, keepdims=True)
        scale_rep[e, pl.ds(base, lib_rows), :] = jnp.broadcast_to(
            lax.rsqrt(total + epsilon), (lib_rows, LANES)
        )
        spectra[e, 1, pl.ds(base, lib_rows), :] = jnp.dot(
            rows, onehot[...], preferred_element_type=jnp.float32
        ).astype(jnp.bfloat16)

    def arrive(at):
        for copy in z_copies(at):
            copy.wait_recv()
        forward(at)

    arrive(1)
    arrive(2)
    prepare(c, y)
    arrive(3)
    arrive(4)

    wide_row = lax.broadcasted_iota(jnp.int32, (blocks, LANES), 0)

    def norm(i, carry):
        part, b = i // (blocks // 2), (i % (blocks // 2)) * 2
        wide = qall[pl.ds(b, 2), part].astype(jnp.float32).reshape(2 * ROWS, depth)
        total = jnp.sum(wide * wide, axis=1, keepdims=True)
        norms[part, pl.ds(pl.multiple_of(b * ROWS, 16), 16), :] = jnp.broadcast_to(
            lax.rsqrt(total + epsilon), (2 * ROWS, LANES)
        )
        return carry

    lax.fori_loop(0, NY * blocks // 2, norm, 0)
    for part in range(NY):
        q_scale[part * blocks:(part + 1) * blocks, :] = spread(
            jnp.where(wide_lane // ROWS == wide_row, norms[part].T[:blocks], 0.0)
        )

    own_up.wait_recv()
    relay_up = piece_copy(piece(down, 0, half), l_sems, 2, (m, up))
    core_down = piece_copy(piece(down), c_sems, 1, (partner, y))
    start((relay_up, core_down))
    own_down.wait_recv()
    relay_down = piece_copy(piece(up, half, half), l_sems, 3, (m, down))
    core_up = piece_copy(piece(up), c_sems, 2, (partner, y))
    start((relay_down, core_up))
    arrive(5)
    own_core.wait_recv()
    prepare(1 - c, y)
    prepare(c, down)
    arrive(6)
    prepare(c, up)
    core_down.wait_recv()
    prepare(1 - c, down)
    arrive(7)
    core_up.wait_recv()
    prepare(1 - c, up)
    relay_up.wait_recv()
    relay_down.wait_recv()
    core_opposite = piece_copy(piece(opposite), c_sems, 3, (partner, y))
    core_opposite.start()
    prepare(c, opposite)

    for copy in lm_copies:
        copy.wait()
    for e in range(NC):
        for at in range(NY):
            mass = jnp.broadcast_to(lmbuf[e, at].astype(jnp.float32), (lib_rows, LANES)).T
            mass = mass + ((x * NC + e) * BINS).astype(jnp.float32) + OFFSET
            mass_rep[e, at * lib_rows:(at + 1) * lib_rows, :] = mass
    core_opposite.wait_recv()
    prepare(1 - c, opposite)

    def pack(at):
        for dx in range(NX):
            for copy in x_copies(at, dx):
                if dx:
                    copy.wait_recv()
                else:
                    copy.wait()
        for slot in range(2):
            for side in range(0, NX, 2):
                rows = qbuf[at, side:side + 2, slot].astype(jnp.float32).reshape(2 * ROWS, depth)
                base = slot * LANES + ((at * NX + side) % 16) * ROWS
                columns[base:base + 16, :] = rows.astype(jnp.bfloat16)
        tile = xcode[at, 0].astype(jnp.float32)
        for dx in range(1, NX):
            tile = tile + xcode[at, dx].astype(jnp.float32)
        return tile

    for lg in range(2):
        first_at = lg * NZ // 2
        combined = pack(first_at)
        for at in range(first_at + 1, first_at + NZ // 2):
            combined = combined + pack(at)

        masses = []
        others = []
        for e in range(NC):
            scores[e] = lax.dot_general(
                spectra[e].reshape(2 * range_rows, depth), columns[...], (((1,), (1,)), ((), ())),
                preferred_element_type=jnp.float32,
            )
            code_row = jnp.sum(jnp.where(row8 == x * NC + e, combined, 0.0), axis=0, keepdims=True)
            code_row = jnp.broadcast_to(code_row, (ROWS, LANES))
            masses.append(jnp.abs(code_row))
            others.append(code_row < 0.0)

        def scan(i, best):
            base = pl.multiple_of(i * ROWS, ROWS)
            found = []
            for e in range(NC):
                scale = scale_rep[e, pl.ds(base, ROWS), :]
                allowed = jnp.abs(masses[e] - mass_rep[e, pl.ds(base, ROWS), :]) <= TOLERANCE
                for kind in range(2):
                    rows = pl.ds(kind * range_rows + base, ROWS)
                    score = jnp.where(others[e], scores[e, rows, LANES:], scores[e, rows, :LANES]) * scale
                    at = (e * 2 + kind) * TOP_HITS
                    found += insert(best[at:at + TOP_HITS], jnp.where(allowed, score, EMPTY))
            return tuple(found)

        nothing = jnp.full((ROWS, LANES), EMPTY, jnp.float32)
        best = lax.fori_loop(
            0, range_rows // ROWS, scan, (nothing,) * (4 * TOP_HITS), unroll=2
        )
        for e in range(NC):
            lanes = []
            for kind in range(2):
                at = (e * 2 + kind) * TOP_HITS
                part = list(best[at:at + TOP_HITS])
                for shift in (4, 2, 1):
                    part = merged(part, [pltpu.roll(v, shift, 0) for v in part])
                lanes += part
            upper = lanes[0]
            for k in range(1, 8):
                upper = jnp.where(row8 == k, lanes[k], upper)
            lower = jnp.where(row8 == 0, lanes[8], lanes[9])
            table = swap_blocks(jnp.concatenate([upper, lower], axis=0))
            for k in range(16):
                obuf[lg * 16 + k, e] = table[k:k + 1, :]

    own_rows = (y * CHIPS + g) * NC
    for at in range(NZ - 1, -1, -1):
        for dx in range(NX):
            chip = turn(z, NZ - ORDER[at], NZ) * NX + turn(x, NX - dx, NX)
            for step in (2, 1, 3, 0):
                if at or dx or step:
                    remote(
                        obuf.at[at * NX + dx], rbuf.at[pl.ds(own_rows, NC)], r_send, r_recv,
                        (chip * NC + c, turn(y, step, NY)),
                    ).start()
    keep = pltpu.make_async_copy(obuf.at[0], rbuf.at[pl.ds(own_rows, NC)], here_sem.at[0])
    keep.start()

    for at in range(NZ):
        if at:
            for copy in z_copies(at):
                copy.wait_send()
        for dx in range(1, NX):
            for copy in x_copies(at, dx):
                copy.wait_send()
    for copy in (own_up, own_down, relay_up, relay_down, own_core, core_down, core_up, core_opposite):
        copy.wait_send()

    keep.wait()
    for sem in (r_send, r_recv):
        others = rbuf.at[pl.ds(0, NC * (NY * CHIPS - 1))]
        pltpu.make_async_copy(others, others, sem).wait()

    for b in range(blocks):
        first = first_ref[b]
        for part in range(NY):
            for w in range(WINDOW):
                row = part * blocks + b
                abuf[w, row:row + 1, :] = rbuf[part * CHIPS * NC + first + w]
    best = None
    for w in range(WINDOW):
        rows = abuf[w]
        parts = [rows] + [pltpu.roll(rows, LANES - ROWS * k, 1) for k in range(1, TOP_HITS)]
        best = parts if best is None else merged(best, parts)
    scale = q_scale[...]
    segment = wide_lane // ROWS
    for k in range(TOP_HITS):
        value = jnp.where(best[k] <= 0.5 * EMPTY, floor_score, best[k] * scale)
        for out, kind in ((out_t, 0), (out_d, TOP_HITS)):
            row = jnp.zeros((blocks, LANES), jnp.float32)
            for part in range(NY):
                moved = value[part * blocks:(part + 1) * blocks]
                shift = (part - kind) * ROWS % LANES
                moved = pltpu.roll(moved, shift, 1) if shift else moved
                row = jnp.where(segment == part, moved, row)
            out[:, k, :] = row[:, :NY * ROWS]


def per_device(queries, query_mass, first_range, library, library_mass, shuffle):
    count, q_rows, depth = queries.shape
    lib_rows = library.shape[0]
    f32, bf16 = jnp.float32, jnp.bfloat16
    vmem = pl.BlockSpec(memory_space=pltpu.VMEM)
    smem = pl.BlockSpec(memory_space=pltpu.SMEM)
    hbm = pl.BlockSpec(memory_space=pl.ANY)
    dma = pltpu.SemaphoreType.DMA
    range_rows = NY * lib_rows
    return tuple(pl.pallas_call(
        search_kernel,
        out_shape=(jax.ShapeDtypeStruct((count, TOP_HITS, q_rows), f32),) * 2,
        in_specs=[smem, hbm, vmem, hbm, hbm, vmem],
        out_specs=(vmem, vmem),
        scratch_shapes=[
            pltpu.VMEM((count, NY, ROWS, depth), bf16),
            pltpu.VMEM((NZ * SLOTS, ROWS, depth), bf16),
            pltpu.VMEM((NZ, ROWS, LANES), bf16),
            pltpu.VMEM((NZ, SLOTS, ROWS, depth), bf16),
            pltpu.VMEM((NZ, ROWS, LANES), bf16),
            pltpu.VMEM((NZ, NX, 2, ROWS, depth), bf16),
            pltpu.VMEM((NZ, NX, ROWS, LANES), bf16),
            pltpu.VMEM((NC, NY, 1, LANES), jnp.int32),
            pltpu.VMEM((NC, 2, range_rows, depth), bf16),
            pltpu.VMEM((depth, depth), bf16),
            pltpu.VMEM((2 * LANES, depth), bf16),
            pltpu.VMEM((NC, range_rows, LANES), f32),
            pltpu.VMEM((NC, range_rows, LANES), f32),
            pltpu.VMEM((NC, 2 * range_rows, 2 * LANES), f32),
            pltpu.VMEM((CHIPS, NC, 1, LANES), f32),
            pltpu.VMEM((NY * CHIPS * NC, 1, LANES), f32),
            pltpu.VMEM((WINDOW, NY * count, LANES), f32),
            pltpu.VMEM((NY, count * ROWS, LANES), f32),
            pltpu.VMEM((NY * count, LANES), f32),
            dma((NZ,)), dma((NZ,)), dma((NZ,)), dma((NZ,)),
            dma((NZ, NX)), dma((NZ, NX)), dma((NZ, NX)), dma((NZ, NX)), dma, dma,
            dma((4,)), dma((4,)), dma((4,)), dma((4,)), dma((8,)), dma((8,)),
            dma((3 + 2 * NZ,)),
        ],
        compiler_params=pltpu.CompilerParams(collective_id=0, has_side_effects=True),
        name="search",
    )(
        first_range, queries.reshape(count, NY, ROWS, depth), query_mass, library,
        library_mass.reshape(1, LANES), shuffle.reshape(1, depth),
    ))


def solution(mesh):
    return jax.shard_map(
        per_device,
        mesh=mesh,
        in_specs=(
            P("mass", None, None),
            P("mass", None),
            P("mass"),
            P(("mass", "sub"), None),
            P(("mass", "sub")),
            P(),
        ),
        out_specs=(P("mass", None, None), P("mass", None, None)),
        check_vma=False,
    )
```

```python
import jax
import jax.numpy as jnp
from jax import lax
from jax.experimental import pallas as pl
from jax.experimental.pallas import tpu as pltpu
from jax.sharding import PartitionSpec as P

BINS = 16
TOLERANCE = 4
WINDOW = 3
TOP_HITS = 5
NZ, NX, NC, NY = 8, 4, 2, 4
CHIPS = NZ * NX
SLOTS = 4
ROWS = 8
LANES = 128
OFFSET = 64.0
epsilon = 1e-06
floor_score = -3.0
EMPTY = -1e30
MESH = pl.DeviceIdType.MESH
ORDER = (0, 1, 7, 2, 6, 3, 5, 4)


def insert(best, new, start=0):
    best = list(best)
    for k in range(start, TOP_HITS):
        high = jnp.maximum(best[k], new)
        if k + 1 < TOP_HITS:
            new = jnp.minimum(best[k], new)
        best[k] = high
    return best


def merged(former, latter):
    for k in range(TOP_HITS):
        former = insert(former, latter[k], k)
    return former


def spread(rows):
    for shift in (8, 16, 32, 64):
        rows = rows + pltpu.roll(rows, shift, 1)
    return rows


def swap_blocks(table):
    row = lax.broadcasted_iota(jnp.int32, table.shape, 0)
    segment = lax.broadcasted_iota(jnp.int32, table.shape, 1) // ROWS
    for bit in range(4):
        step = 1 << bit
        up = pltpu.roll(pltpu.roll(table, 16 - step, 0), ROWS * step, 1)
        down = pltpu.roll(pltpu.roll(table, step, 0), LANES - ROWS * step, 1)
        row_bit = (row // step) % 2
        segment_bit = (segment // step) % 2
        table = jnp.where(row_bit == segment_bit, table, jnp.where(row_bit == 0, up, down))
    return table


def search_kernel(
    first_range, queries, query_mass, lib, lib_mass, shuffle, out,
    first_ref, q_mass, names_ref, qall, send, code, zbuf, zcode, qbuf, xcode, lmbuf, spectra, onehot, columns, scale_rep, mass_rep,
    scores, obuf, rbuf, abuf, norms, q_scale,
    z_send, z_recv, zc_send, zc_recv, x_send, x_recv, xc_send, xc_recv, r_send, r_recv,
    l_send, l_recv, c_send, c_recv, lm_send, lm_recv, here_sem,
):
    m = lax.axis_index("mass")
    y = lax.axis_index("sub")
    blocks = q_mass.shape[0]
    lib_rows, depth = lib.shape
    range_rows = NY * lib_rows
    z = m // (NX * NC)
    x = (m // NC) % NX
    c = m % NC
    g = m // NC
    partner = m + 1 - 2 * c

    def device(chip):
        return (chip * NC + c, y)

    def turn(value, step, count):
        return lax.rem(value + step, count)

    def remote(src, dst, send_sem, recv_sem, target):
        return pltpu.make_async_remote_copy(
            src_ref=src, dst_ref=dst, send_sem=send_sem, recv_sem=recv_sem,
            device_id=target, device_id_type=MESH,
        )

    barrier = pltpu.get_barrier_semaphore()
    peers = [device(turn(z, s, NZ) * NX + x) for s in range(1, NZ)]
    peers += [device(z * NX + turn(x, s, NX)) for s in range(1, NX)]
    peers += [(m, turn(y, s, NY)) for s in range(1, NY)]
    peers += [(partner, turn(y, s, NY)) for s in range(NY)]
    for peer in peers:
        pl.semaphore_signal(barrier, inc=1, device_id=peer, device_id_type=MESH)

    take_first = pltpu.make_async_copy(first_range, first_ref, here_sem.at[3])
    take_q_mass = pltpu.make_async_copy(query_mass, q_mass, here_sem.at[4])
    take_names = pltpu.make_async_copy(shuffle, names_ref, here_sem.at[5])
    for copy in (take_first, take_q_mass, take_names):
        copy.start()
    take_queries = pltpu.make_async_copy(queries, qall, here_sem.at[0])
    take_queries.start()
    own_lib = spectra.at[c, 0, pl.ds(y * lib_rows, lib_rows)]
    take_lib = pltpu.make_async_copy(lib, own_lib, here_sem.at[1])
    take_lib.start()
    take_mass = pltpu.make_async_copy(lib_mass, lmbuf.at[c, y], here_sem.at[2])
    take_mass.start()

    take_first.wait()
    take_q_mass.wait()

    lane = lax.broadcasted_iota(jnp.int32, (ROWS, LANES), 1)
    row8 = lax.broadcasted_iota(jnp.int32, (ROWS, LANES), 0)
    wide_lane = lax.broadcasted_iota(jnp.int32, (blocks, LANES), 1)
    own_mass = jnp.concatenate(
        [q_mass[...].astype(jnp.float32), jnp.zeros((blocks, LANES - NY * ROWS), jnp.float32)], axis=1
    )
    own_mass = pltpu.roll(own_mass, turn(LANES - y * ROWS, 0, LANES), 1)
    own_mass = spread(jnp.where(wide_lane < ROWS, own_mass, 0.0))
    pair_start = jnp.maximum(row8 // 2 - 1, 0)
    for at, dz in enumerate(ORDER):
        base = turn(z, dz, NZ) * (NX * NC)
        ranges = row8 + base
        threshold = base + 3 * pair_start + 1
        tile = jnp.zeros((ROWS, LANES), jnp.float32)
        for b in range(blocks):
            start = first_ref[b]
            shift = ((start - base) * BINS).astype(jnp.float32) + OFFSET
            value = own_mass[b:b + 1, :] + shift
            value = jnp.where(start >= threshold, -value, value)
            ahead = ranges - start
            tile = jnp.where((ahead >= 0) & (ahead < WINDOW), value, tile)
        dx = lax.rem(row8 // 2 - x + NX, NX)
        place = lax.rem(at * NX + dx, 16)
        code[at] = jnp.where(lane // ROWS == place, tile, 0.0).astype(jnp.bfloat16)

    take_queries.wait()

    def gather(i, carry):
        row = i // SLOTS
        low = row * (NX * NC) - 2 + 3 * (i % SLOTS)
        high = jnp.minimum(low + 2, row * (NX * NC) + NX * NC - 1)
        chosen = jnp.int32(0)
        for b in range(blocks):
            start = first_ref[b]
            chosen = jnp.where((start >= low) & (start <= high), b, chosen)
        send[i] = qall[chosen, y]
        return carry

    lax.fori_loop(0, NZ * SLOTS, gather, 0)
    chunk = 64
    take_names.wait()
    names = names_ref[...]

    def build(i, carry):
        base = pl.multiple_of(i * chunk, chunk)
        index = lax.broadcasted_iota(jnp.int32, (chunk, depth), 0) + base
        onehot[pl.ds(base, chunk), :] = jnp.where(index == names, 1.0, 0.0).astype(jnp.bfloat16)
        return carry

    lax.fori_loop(0, depth // chunk, build, 0)

    take_lib.wait()
    take_mass.wait()

    pl.semaphore_wait(barrier, len(peers))

    def z_copies(at):
        zt = turn(z, ORDER[at], NZ)
        target = device(zt * NX + x)
        return (
            remote(send.at[pl.ds(zt * SLOTS, SLOTS)], zbuf.at[at], z_send.at[at], z_recv.at[at], target),
            remote(code.at[at], zcode.at[at], zc_send.at[at], zc_recv.at[at], target),
        )

    def x_copies(at, dx):
        xt = turn(x, dx, NX)
        start = jnp.maximum(xt - 1, 0)
        if at:
            pair, codes = zbuf.at[at, pl.ds(start, 2)], zcode.at[at]
        else:
            pair, codes = send.at[pl.ds(z * SLOTS + start, 2)], code.at[0]
        to_pair, to_codes = qbuf.at[at, dx], xcode.at[at, dx]
        if dx == 0:
            return (
                pltpu.make_async_copy(pair, to_pair, here_sem.at[3 + at]),
                pltpu.make_async_copy(codes, to_codes, here_sem.at[3 + NZ + at]),
            )
        target = device(z * NX + xt)
        return (
            remote(pair, to_pair, x_send.at[at, dx], x_recv.at[at, dx], target),
            remote(codes, to_codes, xc_send.at[at, dx], xc_recv.at[at, dx], target),
        )

    def start(copies):
        for copy in copies:
            copy.start()

    def forward(at):
        for dx in (2, 1, 3, 0):
            start(x_copies(at, dx))

    half = lib_rows // 2
    up, down, opposite = turn(y, 1, NY), turn(y, NY - 1, NY), turn(y, 2, NY)

    def piece(at, first=0, count=lib_rows):
        return spectra.at[c, 0, pl.ds(at * lib_rows + first, count)]

    def piece_copy(part, sems, at, target):
        return remote(part, part, sems[0].at[at], sems[1].at[at], target)

    l_sems, c_sems = (l_send, l_recv), (c_send, c_recv)
    own_up = piece_copy(piece(y), l_sems, 0, (m, up))
    own_down = piece_copy(piece(y), l_sems, 1, (m, down))
    own_core = piece_copy(piece(y), c_sems, 0, (partner, y))
    start((own_up, own_down, own_core))
    for at in range(1, NZ):
        start(z_copies(at))
    forward(0)

    lm_copies = []
    for core in range(NC):
        for step in range(NY):
            if core or step:
                at = core * NY + step
                target = (partner if core else m, turn(y, step, NY))
                lm_copies.append(remote(
                    lmbuf.at[c, y], lmbuf.at[c, y], lm_send.at[at], lm_recv.at[at], target
                ))
    start(lm_copies)

    def prepare(e, at):
        base = pl.multiple_of(at * lib_rows, lib_rows)
        rows = spectra[e, 0, pl.ds(base, lib_rows), :]
        wide = rows.astype(jnp.float32)
        total = jnp.sum(wide * wide, axis=1, keepdims=True)
        scale_rep[e, pl.ds(base, lib_rows), :] = jnp.broadcast_to(
            lax.rsqrt(total + epsilon), (lib_rows, LANES)
        )
        spectra[e, 1, pl.ds(base, lib_rows), :] = jnp.dot(
            rows, onehot[...], preferred_element_type=jnp.float32
        ).astype(jnp.bfloat16)

    def arrive(at):
        for copy in z_copies(at):
            copy.wait_recv()
        forward(at)

    arrive(1)
    arrive(2)
    prepare(c, y)
    arrive(3)
    arrive(4)

    own_up.wait_recv()
    relay_up = piece_copy(piece(down, 0, half), l_sems, 2, (m, up))
    core_down = piece_copy(piece(down), c_sems, 1, (partner, y))
    start((relay_up, core_down))
    own_down.wait_recv()
    relay_down = piece_copy(piece(up, half, half), l_sems, 3, (m, down))
    core_up = piece_copy(piece(up), c_sems, 2, (partner, y))
    start((relay_down, core_up))
    arrive(5)
    own_core.wait_recv()
    prepare(1 - c, y)
    prepare(c, down)
    arrive(6)
    prepare(c, up)
    core_down.wait_recv()
    prepare(1 - c, down)
    relay_up.wait_recv()
    relay_down.wait_recv()
    core_opposite = piece_copy(piece(opposite), c_sems, 3, (partner, y))
    core_opposite.start()
    arrive(7)
    core_up.wait_recv()
    prepare(1 - c, up)
    prepare(c, opposite)

    for copy in lm_copies:
        copy.wait()
    for e in range(NC):
        for at in range(NY):
            mass = jnp.broadcast_to(lmbuf[e, at].astype(jnp.float32), (lib_rows, LANES)).T
            mass = mass + ((x * NC + e) * BINS).astype(jnp.float32) + OFFSET
            mass_rep[e, at * lib_rows:(at + 1) * lib_rows, :] = mass
    core_opposite.wait_recv()
    prepare(1 - c, opposite)

    def pack(at):
        for dx in range(NX):
            for copy in x_copies(at, dx):
                if dx:
                    copy.wait_recv()
                else:
                    copy.wait()
        for slot in range(2):
            for side in range(0, NX, 2):
                rows = qbuf[at, side:side + 2, slot].astype(jnp.float32).reshape(2 * ROWS, depth)
                base = slot * LANES + ((at * NX + side) % 16) * ROWS
                columns[base:base + 16, :] = rows.astype(jnp.bfloat16)
        tile = xcode[at, 0].astype(jnp.float32)
        for dx in range(1, NX):
            tile = tile + xcode[at, dx].astype(jnp.float32)
        return tile

    own_rows = (y * CHIPS + g) * NC

    def give(at):
        for dx in range(NX):
            chip = turn(z, NZ - ORDER[at], NZ) * NX + turn(x, NX - dx, NX)
            for step in (2, 1, 3, 0):
                if at or dx or step:
                    remote(
                        obuf.at[at * NX + dx], rbuf.at[pl.ds(own_rows, NC)], r_send, r_recv,
                        (chip * NC + c, turn(y, step, NY)),
                    ).start()

    for lg in range(2):
        first_at = lg * NZ // 2
        combined = pack(first_at)
        for at in range(first_at + 1, first_at + NZ // 2):
            combined = combined + pack(at)

        masses = []
        others = []
        for e in range(NC):
            scores[e] = lax.dot_general(
                spectra[e].reshape(2 * range_rows, depth), columns[...], (((1,), (1,)), ((), ())),
                preferred_element_type=jnp.float32,
            )
            code_row = jnp.sum(jnp.where(row8 == x * NC + e, combined, 0.0), axis=0, keepdims=True)
            code_row = jnp.broadcast_to(code_row, (ROWS, LANES))
            masses.append(jnp.abs(code_row))
            others.append(code_row < 0.0)

        def scan(i, best):
            base = pl.multiple_of(i * ROWS, ROWS)
            found = []
            for e in range(NC):
                scale = scale_rep[e, pl.ds(base, ROWS), :]
                allowed = jnp.abs(masses[e] - mass_rep[e, pl.ds(base, ROWS), :]) <= TOLERANCE
                for kind in range(2):
                    rows = pl.ds(kind * range_rows + base, ROWS)
                    score = jnp.where(others[e], scores[e, rows, LANES:], scores[e, rows, :LANES]) * scale
                    at = (e * 2 + kind) * TOP_HITS
                    found += insert(best[at:at + TOP_HITS], jnp.where(allowed, score, EMPTY))
            return tuple(found)

        nothing = jnp.full((ROWS, LANES), EMPTY, jnp.float32)
        best = lax.fori_loop(
            0, range_rows // ROWS, scan, (nothing,) * (4 * TOP_HITS), unroll=8
        )
        for e in range(NC):
            lanes = []
            for kind in range(2):
                at = (e * 2 + kind) * TOP_HITS
                part = list(best[at:at + TOP_HITS])
                for shift in (4, 2, 1):
                    part = merged(part, [pltpu.roll(v, shift, 0) for v in part])
                lanes += part
            upper = lanes[0]
            for k in range(1, 8):
                upper = jnp.where(row8 == k, lanes[k], upper)
            lower = jnp.where(row8 == 0, lanes[8], lanes[9])
            table = swap_blocks(jnp.concatenate([upper, lower], axis=0))
            for k in range(16):
                obuf[lg * 16 + k, e] = table[k:k + 1, :]
        for at in range(first_at + NZ // 2 - 1, first_at - 1, -1):
            give(at)

    keep = pltpu.make_async_copy(obuf.at[0], rbuf.at[pl.ds(own_rows, NC)], here_sem.at[0])
    keep.start()

    for at in range(NZ):
        if at:
            for copy in z_copies(at):
                copy.wait_send()
        for dx in range(1, NX):
            for copy in x_copies(at, dx):
                copy.wait_send()
    for copy in (own_up, own_down, relay_up, relay_down, own_core, core_down, core_up, core_opposite):
        copy.wait_send()

    wide_row = lax.broadcasted_iota(jnp.int32, (blocks, LANES), 0)

    def norm(i, carry):
        part, b = i // (blocks // 2), (i % (blocks // 2)) * 2
        wide = qall[pl.ds(b, 2), part].astype(jnp.float32).reshape(2 * ROWS, depth)
        total = jnp.sum(wide * wide, axis=1, keepdims=True)
        norms[part, pl.ds(pl.multiple_of(b * ROWS, 16), 16), :] = jnp.broadcast_to(
            lax.rsqrt(total + epsilon), (2 * ROWS, LANES)
        )
        return carry

    lax.fori_loop(0, NY * blocks // 2, norm, 0)
    for part in range(NY):
        q_scale[part * blocks:(part + 1) * blocks, :] = spread(
            jnp.where(wide_lane // ROWS == wide_row, norms[part].T[:blocks], 0.0)
        )

    keep.wait()
    for sem in (r_send, r_recv):
        others = rbuf.at[pl.ds(0, NC * (NY * CHIPS - 1))]
        pltpu.make_async_copy(others, others, sem).wait()

    for b in range(blocks):
        first = first_ref[b]
        for part in range(NY):
            for w in range(WINDOW):
                row = part * blocks + b
                abuf[w, row:row + 1, :] = rbuf[part * CHIPS * NC + first + w]
    best = None
    for w in range(WINDOW):
        rows = abuf[w]
        parts = [rows] + [pltpu.roll(rows, LANES - ROWS * k, 1) for k in range(1, TOP_HITS)]
        best = parts if best is None else merged(best, parts)
    scale = q_scale[...]
    segment = wide_lane // ROWS
    for k in range(TOP_HITS):
        value = jnp.where(best[k] <= 0.5 * EMPTY, floor_score, best[k] * scale)
        for side in range(2):
            row = jnp.zeros((blocks, LANES), jnp.float32)
            for part in range(NY):
                moved = value[part * blocks:(part + 1) * blocks]
                shift = (part - side * TOP_HITS) * ROWS % LANES
                moved = pltpu.roll(moved, shift, 1) if shift else moved
                row = jnp.where(segment == part, moved, row)
            out[side, k] = row[:, :NY * ROWS]


def per_device(queries, query_mass, first_range, library, library_mass, shuffle):
    count, q_rows, depth = queries.shape
    lib_rows = library.shape[0]
    f32, bf16 = jnp.float32, jnp.bfloat16
    vmem = pl.BlockSpec(memory_space=pltpu.VMEM)
    hbm = pl.BlockSpec(memory_space=pl.ANY)
    dma = pltpu.SemaphoreType.DMA
    range_rows = NY * lib_rows
    found = pl.pallas_call(
        search_kernel,
        out_shape=jax.ShapeDtypeStruct((2, TOP_HITS, count, q_rows), f32),
        in_specs=[hbm] * 6,
        out_specs=vmem,
        scratch_shapes=[
            pltpu.SMEM((count,), jnp.int32),
            pltpu.VMEM((count, q_rows), jnp.int32),
            pltpu.VMEM((1, depth), jnp.int32),
            pltpu.VMEM((count, NY, ROWS, depth), bf16),
            pltpu.VMEM((NZ * SLOTS, ROWS, depth), bf16),
            pltpu.VMEM((NZ, ROWS, LANES), bf16),
            pltpu.VMEM((NZ, SLOTS, ROWS, depth), bf16),
            pltpu.VMEM((NZ, ROWS, LANES), bf16),
            pltpu.VMEM((NZ, NX, 2, ROWS, depth), bf16),
            pltpu.VMEM((NZ, NX, ROWS, LANES), bf16),
            pltpu.VMEM((NC, NY, 1, LANES), jnp.int32),
            pltpu.VMEM((NC, 2, range_rows, depth), bf16),
            pltpu.VMEM((depth, depth), bf16),
            pltpu.VMEM((2 * LANES, depth), bf16),
            pltpu.VMEM((NC, range_rows, LANES), f32),
            pltpu.VMEM((NC, range_rows, LANES), f32),
            pltpu.VMEM((NC, 2 * range_rows, 2 * LANES), f32),
            pltpu.VMEM((CHIPS, NC, 1, LANES), f32),
            pltpu.VMEM((NY * CHIPS * NC, 1, LANES), f32),
            pltpu.VMEM((WINDOW, NY * count, LANES), f32),
            pltpu.VMEM((NY, count * ROWS, LANES), f32),
            pltpu.VMEM((NY * count, LANES), f32),
            dma((NZ,)), dma((NZ,)), dma((NZ,)), dma((NZ,)),
            dma((NZ, NX)), dma((NZ, NX)), dma((NZ, NX)), dma((NZ, NX)), dma, dma,
            dma((4,)), dma((4,)), dma((4,)), dma((4,)), dma((8,)), dma((8,)),
            dma((3 + 2 * NZ,)),
        ],
        compiler_params=pltpu.CompilerParams(collective_id=0, has_side_effects=True),
        name="search",
    )(
        first_range, queries.reshape(count, NY, ROWS, depth), query_mass, library,
        library_mass.reshape(1, LANES), shuffle.reshape(1, depth),
    )
    def settle(hits, out_t, out_d, held, sem_in, sem_out):
        copy = pltpu.make_async_copy(hits, held, sem_in)
        copy.start()
        copy.wait()
        copies = [
            pltpu.make_async_copy(held.at[side], out, sem_out.at[side])
            for side, out in enumerate((out_t, out_d))
        ]
        for copy in copies:
            copy.start()
        for copy in copies:
            copy.wait()

    parts = pl.pallas_call(
        settle,
        out_shape=(jax.ShapeDtypeStruct((TOP_HITS, count, q_rows), f32),) * 2,
        in_specs=[hbm], out_specs=(hbm, hbm),
        scratch_shapes=[pltpu.VMEM((2, TOP_HITS, count, q_rows), f32), dma, dma((2,))],
        name="settle",
    )(found)
    return tuple(jnp.transpose(part, (1, 0, 2)) for part in parts)


def solution(mesh):
    return jax.shard_map(
        per_device,
        mesh=mesh,
        in_specs=(
            P("mass", None, None),
            P("mass", None),
            P("mass"),
            P(("mass", "sub"), None),
            P(("mass", "sub")),
            P(),
        ),
        out_specs=(P("mass", None, None), P("mass", None, None)),
        check_vma=False,
    )
```

```python
import jax
import jax.numpy as jnp
from jax import lax
from jax.experimental import pallas as pl
from jax.experimental.pallas import tpu as pltpu
from jax.sharding import PartitionSpec as P

BINS = 16
TOLERANCE = 4
WINDOW = 3
TOP_HITS = 5
NZ, NX, NC, NY = 8, 4, 2, 4
CHIPS = NZ * NX
SLOTS = 4
ROWS = 8
LANES = 128
OFFSET = 64.0
epsilon = 1e-06
floor_score = -3.0
EMPTY = -1e30
MESH = pl.DeviceIdType.MESH
ORDER = (0, 1, 7, 2, 6, 3, 5, 4)


def insert(best, new, start=0):
    best = list(best)
    for k in range(start, TOP_HITS):
        high = jnp.maximum(best[k], new)
        if k + 1 < TOP_HITS:
            new = jnp.minimum(best[k], new)
        best[k] = high
    return best


def merged(former, latter):
    for k in range(TOP_HITS):
        former = insert(former, latter[k], k)
    return former


def spread(rows):
    for shift in (8, 16, 32, 64):
        rows = rows + pltpu.roll(rows, shift, 1)
    return rows


def swap_blocks(table):
    row = lax.broadcasted_iota(jnp.int32, table.shape, 0)
    segment = lax.broadcasted_iota(jnp.int32, table.shape, 1) // ROWS
    for bit in range(4):
        step = 1 << bit
        up = pltpu.roll(pltpu.roll(table, 16 - step, 0), ROWS * step, 1)
        down = pltpu.roll(pltpu.roll(table, step, 0), LANES - ROWS * step, 1)
        row_bit = (row // step) % 2
        segment_bit = (segment // step) % 2
        table = jnp.where(row_bit == segment_bit, table, jnp.where(row_bit == 0, up, down))
    return table


def search_kernel(
    first_range, queries, query_mass, lib, lib_mass, shuffle, out,
    first_ref, q_mass, names_ref, qall, send, code, zbuf, zcode, qbuf, xcode, lmbuf, spectra, onehot, columns, scale_rep, mass_rep,
    scores, obuf, rbuf, abuf, norms, q_scale,
    z_send, z_recv, zc_send, zc_recv, x_send, x_recv, xc_send, xc_recv, r_send, r_recv,
    l_send, l_recv, c_send, c_recv, lm_send, lm_recv, here_sem,
):
    m = lax.axis_index("mass")
    y = lax.axis_index("sub")
    blocks = q_mass.shape[0]
    lib_rows, depth = lib.shape
    range_rows = NY * lib_rows
    z = m // (NX * NC)
    x = (m // NC) % NX
    c = m % NC
    g = m // NC
    partner = m + 1 - 2 * c

    def device(chip):
        return (chip * NC + c, y)

    def turn(value, step, count):
        return lax.rem(value + step, count)

    def remote(src, dst, send_sem, recv_sem, target):
        return pltpu.make_async_remote_copy(
            src_ref=src, dst_ref=dst, send_sem=send_sem, recv_sem=recv_sem,
            device_id=target, device_id_type=MESH,
        )

    barrier = pltpu.get_barrier_semaphore()
    peers = [device(turn(z, s, NZ) * NX + x) for s in range(1, NZ)]
    peers += [device(z * NX + turn(x, s, NX)) for s in range(1, NX)]
    peers += [(m, turn(y, s, NY)) for s in range(1, NY)]
    peers += [(partner, turn(y, s, NY)) for s in range(NY)]
    for peer in peers:
        pl.semaphore_signal(barrier, inc=1, device_id=peer, device_id_type=MESH)

    take_first = pltpu.make_async_copy(first_range, first_ref, here_sem.at[3])
    take_q_mass = pltpu.make_async_copy(query_mass, q_mass, here_sem.at[4])
    take_names = pltpu.make_async_copy(shuffle, names_ref, here_sem.at[5])
    for copy in (take_first, take_q_mass, take_names):
        copy.start()
    take_queries = pltpu.make_async_copy(queries, qall, here_sem.at[0])
    take_queries.start()
    own_lib = spectra.at[c, 0, pl.ds(y * lib_rows, lib_rows)]
    take_lib = pltpu.make_async_copy(lib, own_lib, here_sem.at[1])
    take_lib.start()
    take_mass = pltpu.make_async_copy(lib_mass, lmbuf.at[c, y], here_sem.at[2])
    take_mass.start()

    take_first.wait()
    take_q_mass.wait()

    lane = lax.broadcasted_iota(jnp.int32, (ROWS, LANES), 1)
    row8 = lax.broadcasted_iota(jnp.int32, (ROWS, LANES), 0)
    wide_lane = lax.broadcasted_iota(jnp.int32, (blocks, LANES), 1)
    own_mass = jnp.concatenate(
        [q_mass[...].astype(jnp.float32), jnp.zeros((blocks, LANES - NY * ROWS), jnp.float32)], axis=1
    )
    own_mass = pltpu.roll(own_mass, turn(LANES - y * ROWS, 0, LANES), 1)
    own_mass = spread(jnp.where(wide_lane < ROWS, own_mass, 0.0))
    pair_start = jnp.maximum(row8 // 2 - 1, 0)
    for at, dz in enumerate(ORDER):
        base = turn(z, dz, NZ) * (NX * NC)
        ranges = row8 + base
        threshold = base + 3 * pair_start + 1
        tile = jnp.zeros((ROWS, LANES), jnp.float32)
        for b in range(blocks):
            start = first_ref[b]
            shift = ((start - base) * BINS).astype(jnp.float32) + OFFSET
            value = own_mass[b:b + 1, :] + shift
            value = jnp.where(start >= threshold, -value, value)
            ahead = ranges - start
            tile = jnp.where((ahead >= 0) & (ahead < WINDOW), value, tile)
        dx = lax.rem(row8 // 2 - x + NX, NX)
        place = lax.rem(at * NX + dx, 16)
        code[at] = jnp.where(lane // ROWS == place, tile, 0.0).astype(jnp.bfloat16)

    take_queries.wait()

    def gather(i, carry):
        row = i // SLOTS
        low = row * (NX * NC) - 2 + 3 * (i % SLOTS)
        high = jnp.minimum(low + 2, row * (NX * NC) + NX * NC - 1)
        chosen = jnp.int32(0)
        for b in range(blocks):
            start = first_ref[b]
            chosen = jnp.where((start >= low) & (start <= high), b, chosen)
        send[i] = qall[chosen, y]
        return carry

    lax.fori_loop(0, NZ * SLOTS, gather, 0)
    chunk = 64
    take_names.wait()
    names = names_ref[...]

    def build(i, carry):
        base = pl.multiple_of(i * chunk, chunk)
        index = lax.broadcasted_iota(jnp.int32, (chunk, depth), 0) + base
        onehot[pl.ds(base, chunk), :] = jnp.where(index == names, 1.0, 0.0).astype(jnp.bfloat16)
        return carry

    lax.fori_loop(0, depth // chunk, build, 0)

    take_lib.wait()
    take_mass.wait()

    pl.semaphore_wait(barrier, len(peers))

    def z_copies(at):
        zt = turn(z, ORDER[at], NZ)
        target = device(zt * NX + x)
        return (
            remote(send.at[pl.ds(zt * SLOTS, SLOTS)], zbuf.at[at], z_send.at[at], z_recv.at[at], target),
            remote(code.at[at], zcode.at[at], zc_send.at[at], zc_recv.at[at], target),
        )

    def x_copies(at, dx):
        xt = turn(x, dx, NX)
        start = jnp.maximum(xt - 1, 0)
        if at:
            pair, codes = zbuf.at[at, pl.ds(start, 2)], zcode.at[at]
        else:
            pair, codes = send.at[pl.ds(z * SLOTS + start, 2)], code.at[0]
        to_pair, to_codes = qbuf.at[at, dx], xcode.at[at, dx]
        if dx == 0:
            return (
                pltpu.make_async_copy(pair, to_pair, here_sem.at[3 + at]),
                pltpu.make_async_copy(codes, to_codes, here_sem.at[3 + NZ + at]),
            )
        target = device(z * NX + xt)
        return (
            remote(pair, to_pair, x_send.at[at, dx], x_recv.at[at, dx], target),
            remote(codes, to_codes, xc_send.at[at, dx], xc_recv.at[at, dx], target),
        )

    def start(copies):
        for copy in copies:
            copy.start()

    def forward(at):
        for dx in (2, 1, 3, 0):
            start(x_copies(at, dx))

    half = lib_rows // 2
    up, down, opposite = turn(y, 1, NY), turn(y, NY - 1, NY), turn(y, 2, NY)

    def piece(at, first=0, count=lib_rows):
        return spectra.at[c, 0, pl.ds(at * lib_rows + first, count)]

    def piece_copy(part, sems, at, target):
        return remote(part, part, sems[0].at[at], sems[1].at[at], target)

    l_sems, c_sems = (l_send, l_recv), (c_send, c_recv)
    own_up = piece_copy(piece(y), l_sems, 0, (m, up))
    own_down = piece_copy(piece(y), l_sems, 1, (m, down))
    own_core = piece_copy(piece(y), c_sems, 0, (partner, y))
    start((own_up, own_down, own_core))
    for at in range(1, NZ):
        start(z_copies(at))
    forward(0)

    lm_copies = []
    for core in range(NC):
        for step in range(NY):
            if core or step:
                at = core * NY + step
                target = (partner if core else m, turn(y, step, NY))
                lm_copies.append(remote(
                    lmbuf.at[c, y], lmbuf.at[c, y], lm_send.at[at], lm_recv.at[at], target
                ))
    start(lm_copies)

    def prepare(e, at):
        base = pl.multiple_of(at * lib_rows, lib_rows)
        rows = spectra[e, 0, pl.ds(base, lib_rows), :]
        wide = rows.astype(jnp.float32)
        total = jnp.sum(wide * wide, axis=1, keepdims=True)
        scale_rep[e, pl.ds(base, lib_rows), :] = jnp.broadcast_to(
            lax.rsqrt(total + epsilon), (lib_rows, LANES)
        )
        spectra[e, 1, pl.ds(base, lib_rows), :] = jnp.dot(
            rows, onehot[...], preferred_element_type=jnp.float32
        ).astype(jnp.bfloat16)

    def arrive(at):
        for copy in z_copies(at):
            copy.wait_recv()
        forward(at)

    arrive(1)
    arrive(2)
    prepare(c, y)
    arrive(3)
    arrive(4)

    own_up.wait_recv()
    relay_up = piece_copy(piece(down, 0, half), l_sems, 2, (m, up))
    core_down = piece_copy(piece(down), c_sems, 1, (partner, y))
    start((relay_up, core_down))
    own_down.wait_recv()
    relay_down = piece_copy(piece(up, half, half), l_sems, 3, (m, down))
    core_up = piece_copy(piece(up), c_sems, 2, (partner, y))
    start((relay_down, core_up))
    arrive(5)
    own_core.wait_recv()
    prepare(1 - c, y)
    prepare(c, down)
    relay_up.wait_recv()
    relay_down.wait_recv()
    core_opposite = piece_copy(piece(opposite), c_sems, 3, (partner, y))
    core_opposite.start()
    arrive(6)
    prepare(c, up)
    core_down.wait_recv()
    prepare(1 - c, down)
    arrive(7)
    core_up.wait_recv()
    prepare(1 - c, up)
    prepare(c, opposite)

    for copy in lm_copies:
        copy.wait()
    for e in range(NC):
        for at in range(NY):
            mass = jnp.broadcast_to(lmbuf[e, at].astype(jnp.float32), (lib_rows, LANES)).T
            mass = mass + ((x * NC + e) * BINS).astype(jnp.float32) + OFFSET
            mass_rep[e, at * lib_rows:(at + 1) * lib_rows, :] = mass
    def pack(at):
        for dx in range(NX):
            for copy in x_copies(at, dx):
                if dx:
                    copy.wait_recv()
                else:
                    copy.wait()
        for slot in range(2):
            for side in range(0, NX, 2):
                rows = qbuf[at, side:side + 2, slot].astype(jnp.float32).reshape(2 * ROWS, depth)
                base = slot * LANES + ((at * NX + side) % 16) * ROWS
                columns[base:base + 16, :] = rows.astype(jnp.bfloat16)
        tile = xcode[at, 0].astype(jnp.float32)
        for dx in range(1, NX):
            tile = tile + xcode[at, dx].astype(jnp.float32)
        return tile

    early = pack(0) + pack(1) + pack(2) + pack(3)
    core_opposite.wait_recv()
    prepare(1 - c, opposite)

    own_rows = (y * CHIPS + g) * NC

    def give(at):
        for dx in range(NX):
            chip = turn(z, NZ - ORDER[at], NZ) * NX + turn(x, NX - dx, NX)
            for step in (2, 1, 3, 0):
                if at or dx or step:
                    remote(
                        obuf.at[at * NX + dx], rbuf.at[pl.ds(own_rows, NC)], r_send, r_recv,
                        (chip * NC + c, turn(y, step, NY)),
                    ).start()

    for lg in range(2):
        first_at = lg * NZ // 2
        combined = pack(4) + pack(5) + pack(6) + pack(7) if lg else early

        masses = []
        others = []
        for e in range(NC):
            scores[e] = lax.dot_general(
                spectra[e].reshape(2 * range_rows, depth), columns[...], (((1,), (1,)), ((), ())),
                preferred_element_type=jnp.float32,
            )
            code_row = jnp.sum(jnp.where(row8 == x * NC + e, combined, 0.0), axis=0, keepdims=True)
            code_row = jnp.broadcast_to(code_row, (ROWS, LANES))
            masses.append(jnp.abs(code_row))
            others.append(code_row < 0.0)

        def scan(i, best):
            base = pl.multiple_of(i * ROWS, ROWS)
            found = []
            for e in range(NC):
                scale = scale_rep[e, pl.ds(base, ROWS), :]
                allowed = jnp.abs(masses[e] - mass_rep[e, pl.ds(base, ROWS), :]) <= TOLERANCE
                for kind in range(2):
                    rows = pl.ds(kind * range_rows + base, ROWS)
                    score = jnp.where(others[e], scores[e, rows, LANES:], scores[e, rows, :LANES]) * scale
                    at = (e * 2 + kind) * TOP_HITS
                    found += insert(best[at:at + TOP_HITS], jnp.where(allowed, score, EMPTY))
            return tuple(found)

        nothing = jnp.full((ROWS, LANES), EMPTY, jnp.float32)
        best = lax.fori_loop(
            0, range_rows // ROWS, scan, (nothing,) * (4 * TOP_HITS), unroll=8
        )
        for e in range(NC):
            lanes = []
            for kind in range(2):
                at = (e * 2 + kind) * TOP_HITS
                part = list(best[at:at + TOP_HITS])
                for shift in (4, 2, 1):
                    part = merged(part, [pltpu.roll(v, shift, 0) for v in part])
                lanes += part
            upper = lanes[0]
            for k in range(1, 8):
                upper = jnp.where(row8 == k, lanes[k], upper)
            lower = jnp.where(row8 == 0, lanes[8], lanes[9])
            table = swap_blocks(jnp.concatenate([upper, lower], axis=0))
            for k in range(16):
                obuf[lg * 16 + k, e] = table[k:k + 1, :]

    for at in range(NZ - 1, -1, -1):
        give(at)
    keep = pltpu.make_async_copy(obuf.at[0], rbuf.at[pl.ds(own_rows, NC)], here_sem.at[0])
    keep.start()

    for at in range(NZ):
        if at:
            for copy in z_copies(at):
                copy.wait_send()
        for dx in range(1, NX):
            for copy in x_copies(at, dx):
                copy.wait_send()
    for copy in (own_up, own_down, relay_up, relay_down, own_core, core_down, core_up, core_opposite):
        copy.wait_send()

    wide_row = lax.broadcasted_iota(jnp.int32, (blocks, LANES), 0)

    def norm(i, carry):
        part, b = i // (blocks // 2), (i % (blocks // 2)) * 2
        wide = qall[pl.ds(b, 2), part].astype(jnp.float32).reshape(2 * ROWS, depth)
        total = jnp.sum(wide * wide, axis=1, keepdims=True)
        norms[part, pl.ds(pl.multiple_of(b * ROWS, 16), 16), :] = jnp.broadcast_to(
            lax.rsqrt(total + epsilon), (2 * ROWS, LANES)
        )
        return carry

    lax.fori_loop(0, NY * blocks // 2, norm, 0)
    for part in range(NY):
        q_scale[part * blocks:(part + 1) * blocks, :] = spread(
            jnp.where(wide_lane // ROWS == wide_row, norms[part].T[:blocks], 0.0)
        )

    keep.wait()
    for sem in (r_send, r_recv):
        others = rbuf.at[pl.ds(0, NC * (NY * CHIPS - 1))]
        pltpu.make_async_copy(others, others, sem).wait()

    for b in range(blocks):
        first = first_ref[b]
        for part in range(NY):
            for w in range(WINDOW):
                row = part * blocks + b
                abuf[w, row:row + 1, :] = rbuf[part * CHIPS * NC + first + w]
    best = None
    for w in range(WINDOW):
        rows = abuf[w]
        parts = [rows] + [pltpu.roll(rows, LANES - ROWS * k, 1) for k in range(1, TOP_HITS)]
        best = parts if best is None else merged(best, parts)
    scale = q_scale[...]
    segment = wide_lane // ROWS
    for k in range(TOP_HITS):
        value = jnp.where(best[k] <= 0.5 * EMPTY, floor_score, best[k] * scale)
        for side in range(2):
            row = jnp.zeros((blocks, LANES), jnp.float32)
            for part in range(NY):
                moved = value[part * blocks:(part + 1) * blocks]
                shift = (part - side * TOP_HITS) * ROWS % LANES
                moved = pltpu.roll(moved, shift, 1) if shift else moved
                row = jnp.where(segment == part, moved, row)
            out[side, k] = row[:, :NY * ROWS]


def per_device(queries, query_mass, first_range, library, library_mass, shuffle):
    count, q_rows, depth = queries.shape
    lib_rows = library.shape[0]
    f32, bf16 = jnp.float32, jnp.bfloat16
    vmem = pl.BlockSpec(memory_space=pltpu.VMEM)
    hbm = pl.BlockSpec(memory_space=pl.ANY)
    dma = pltpu.SemaphoreType.DMA
    range_rows = NY * lib_rows
    found = pl.pallas_call(
        search_kernel,
        out_shape=jax.ShapeDtypeStruct((2, TOP_HITS, count, q_rows), f32),
        in_specs=[hbm] * 6,
        out_specs=vmem,
        scratch_shapes=[
            pltpu.SMEM((count,), jnp.int32),
            pltpu.VMEM((count, q_rows), jnp.int32),
            pltpu.VMEM((1, depth), jnp.int32),
            pltpu.VMEM((count, NY, ROWS, depth), bf16),
            pltpu.VMEM((NZ * SLOTS, ROWS, depth), bf16),
            pltpu.VMEM((NZ, ROWS, LANES), bf16),
            pltpu.VMEM((NZ, SLOTS, ROWS, depth), bf16),
            pltpu.VMEM((NZ, ROWS, LANES), bf16),
            pltpu.VMEM((NZ, NX, 2, ROWS, depth), bf16),
            pltpu.VMEM((NZ, NX, ROWS, LANES), bf16),
            pltpu.VMEM((NC, NY, 1, LANES), jnp.int32),
            pltpu.VMEM((NC, 2, range_rows, depth), bf16),
            pltpu.VMEM((depth, depth), bf16),
            pltpu.VMEM((2 * LANES, depth), bf16),
            pltpu.VMEM((NC, range_rows, LANES), f32),
            pltpu.VMEM((NC, range_rows, LANES), f32),
            pltpu.VMEM((NC, 2 * range_rows, 2 * LANES), f32),
            pltpu.VMEM((CHIPS, NC, 1, LANES), f32),
            pltpu.VMEM((NY * CHIPS * NC, 1, LANES), f32),
            pltpu.VMEM((WINDOW, NY * count, LANES), f32),
            pltpu.VMEM((NY, count * ROWS, LANES), f32),
            pltpu.VMEM((NY * count, LANES), f32),
            dma((NZ,)), dma((NZ,)), dma((NZ,)), dma((NZ,)),
            dma((NZ, NX)), dma((NZ, NX)), dma((NZ, NX)), dma((NZ, NX)), dma, dma,
            dma((4,)), dma((4,)), dma((4,)), dma((4,)), dma((8,)), dma((8,)),
            dma((3 + 2 * NZ,)),
        ],
        compiler_params=pltpu.CompilerParams(collective_id=0, has_side_effects=True),
        name="search",
    )(
        first_range, queries.reshape(count, NY, ROWS, depth), query_mass, library,
        library_mass.reshape(1, LANES), shuffle.reshape(1, depth),
    )
    def settle(hits, out_t, out_d, held, sem_in, sem_out):
        copy = pltpu.make_async_copy(hits, held, sem_in)
        copy.start()
        copy.wait()
        copies = [
            pltpu.make_async_copy(held.at[side], out, sem_out.at[side])
            for side, out in enumerate((out_t, out_d))
        ]
        for copy in copies:
            copy.start()
        for copy in copies:
            copy.wait()

    parts = pl.pallas_call(
        settle,
        out_shape=(jax.ShapeDtypeStruct((TOP_HITS, count, q_rows), f32),) * 2,
        in_specs=[hbm], out_specs=(hbm, hbm),
        scratch_shapes=[pltpu.VMEM((2, TOP_HITS, count, q_rows), f32), dma, dma((2,))],
        name="settle",
    )(found)
    return tuple(jnp.transpose(part, (1, 0, 2)) for part in parts)


def solution(mesh):
    return jax.shard_map(
        per_device,
        mesh=mesh,
        in_specs=(
            P("mass", None, None),
            P("mass", None),
            P("mass"),
            P(("mass", "sub"), None),
            P(("mass", "sub")),
            P(),
        ),
        out_specs=(P("mass", None, None), P("mass", None, None)),
        check_vma=False,
    )
```
